128 devices in a mesh: pool: 4 (over x_hi, core), dp: 32 (over z, x_lo, y).
Axes of the slice: x: 4 (x_hi: 2, x_lo: 2; x = x_hi * 2 + x_lo), y: 4, z: 4, core: 2. Of those that a mesh axis runs over, the one named last changes fastest.
Arguments:
- queries: bfloat16 [4, 32, 256, 2048], P('pool', 'dp'), may hold values from -48 to 48
- cotangent: bfloat16 [4, 32, 256, 2048], P('pool', 'dp'), may hold values from -6 to 6
- cond: bfloat16 [4, 32, 4, 512], P('pool', 'dp'), may hold values from -6 to 6
- nbr_owner: int32 [4, 32, 4, 2], P('pool', 'dp'), may hold values from 0 to 31, as said below
- nbr_block: int32 [4, 32, 4, 2], P('pool', 'dp'), may hold values from 0 to 15
- database: bfloat16 [4, 32, 16, 128, 512], P('pool', 'dp'), may hold values from -6 to 6
- lengths: int32 [4, 32, 16], P('pool', 'dp'), may hold values from 1 to 128, as said below
- gain: float32 [512], replicated, may hold values from 0.25 to 1.75
- w_down: bfloat16 [512, 256], replicated, may hold values from -0.25 to 0.25
- w_up: bfloat16 [256, 512], replicated, may hold values from -0.375 to 0.375
- w_kv: bfloat16 [512, 4096], replicated, may hold values from -0.25 to 0.25
Outputs:
- attn_out: bfloat16 [4, 32, 256, 2048], P('pool', 'dp')
- q_grad: bfloat16 [4, 32, 256, 2048], P('pool', 'dp')
- cond_grad: float32 [4, 32, 4, 512], P('pool', 'dp')
- adapter_grad: float32 [512, 512], P(('pool', 'dp'))
The draws below stay inside these ranges and needn't reach their ends.
Inputs may be any that keep to these rules, and one draw needn't show every extreme that they name: `nbr_owner`: among the 8 neighbours of each of the decoder devices (pool index below 4-1) that share one index of dp, no encoder device is named more than 2 times, and one encoder device, the same for every index of dp, is named exactly 2 times. Entries at pool index 4-1 are not read. `lengths`: every encoder device holds a block of length 128.
All inputs are finite; a program needn't handle non-finite values.
Results may differ from the reference program's by a relative error of at most 0.013.
The reference program's roundings to bfloat16 on the way count: a program that leaves them out, or rounds other values in their place, can miss the bound.
Values may be sent and summed in bfloat16 or wider, within the bound.
A program may use at most 192 MiB of HBM per device.

```python
import jax
import jax.numpy as jnp
from jax import lax

HEADS = 16
HEAD = 128
E = 512
RANK = 256
SPAN = 64
NBR = 2
NLEN = 128
SPANS_DEV = 4
BLK_DEV = 16
HQ = 2048
TOK_DEV = 256
NB_DEV = 8
CAP = 2
N_POOL = 4
N_DP = 32


def draw_queries(key, part):
    normal_part = jnp.clip(jax.random.normal(jax.random.fold_in(key, 1), (N_POOL, N_DP, TOK_DEV, HEADS, HEAD), jnp.float32), -6.0, 6.0)
    return normal_part.reshape(N_POOL, N_DP, TOK_DEV, HEADS * HEAD).astype(jnp.bfloat16)


def draw_nbr_owner(key, part):
    live_count = (N_POOL - 1) * SPANS_DEV * NBR
    slot_count = N_DP * CAP
    full_owner = jax.random.randint(jax.random.fold_in(key, 11), (), 0, N_DP)
    slot_ids = jnp.arange(slot_count, dtype=jnp.int32)

    def column(column_key):
        shuffled = jax.random.permutation(jax.random.fold_in(column_key, 1), slot_count)
        ranked = jnp.argsort(shuffled).astype(jnp.int32)
        priority = jnp.where(slot_ids // CAP == full_owner, slot_ids % CAP, CAP + ranked)
        chosen = jnp.argsort(priority)[:live_count].astype(jnp.int32)
        placed = jax.random.permutation(jax.random.fold_in(column_key, 2), live_count)
        owners_live = (chosen // CAP)[placed]
        spare_rows = jax.random.randint(jax.random.fold_in(column_key, 3), (SPANS_DEV * NBR,), 0, N_DP)
        return jnp.concatenate([owners_live, spare_rows]).astype(jnp.int32).reshape(N_POOL, SPANS_DEV, NBR)
    column_keys = jax.random.split(jax.random.fold_in(key, 5), N_DP)
    return jnp.transpose(jax.vmap(column)(column_keys), (1, 0, 2, 3))


def draw_lengths(key, part):
    drawn = jax.random.randint(jax.random.fold_in(key, 1), (N_POOL, N_DP, BLK_DEV), 1, NLEN + 1)
    longest = jax.random.randint(jax.random.fold_in(key, 2), (N_POOL, N_DP, 1), 0, BLK_DEV)
    position = jnp.arange(BLK_DEV, dtype=jnp.int32)[None, None, :]
    return jnp.where(position == longest, NLEN, drawn).astype(jnp.int32)


def set_ends(array, rng, least, largest):
    dims = array.shape
    spot = [jax.random.randint(jax.random.fold_in(rng, axis), (), 0, dims[axis]) for axis in range(len(dims))]
    array = array.at[tuple(spot)].set(least)
    longest = dims.index(max(dims))
    spot[longest] = (spot[longest] + 1) % dims[longest]
    return array.at[tuple(spot)].set(largest)


def block_scale(key, dims, cuts, low, top_value):
    factor_of = 1.0
    for dim, parts in cuts:
        draws = jax.random.uniform(jax.random.fold_in(jax.random.fold_in(key, 6), dim), (parts,), jnp.float32, low / len(cuts), top_value / len(cuts))
        factor_of = factor_of * jnp.repeat(jnp.exp(draws), dims[dim] // parts).reshape((-1,) + (1,) * (len(dims) - 1 - dim))
    return factor_of


def centred(rng, dims, spread, most, pieces=(), kind=jnp.bfloat16):
    level = block_scale(rng, dims, pieces, -0.22, 0.18) if pieces else 1.0
    entries = jax.random.normal(rng, dims, jnp.float32) * spread * level
    return jnp.minimum(jnp.maximum(entries, -most), most).astype(kind)


def setup_inputs(seed: int = 0) -> dict:
    key_list = jax.random.split(jax.random.key(seed), 12)
    return {
        "queries": draw_queries(jax.random.fold_in(key_list[11], 71), 0),
        "cotangent": centred(key_list[1], (N_POOL, N_DP, TOK_DEV, HQ), 1.0, 6.0, ((0, 4), (1, 32))),
        "cond": centred(key_list[2], (N_POOL, N_DP, SPANS_DEV, E), 1.0, 6.0, ((0, 4), (1, 32))),
        "nbr_owner": draw_nbr_owner(jax.random.fold_in(key_list[11], 71), 0),
        "nbr_block": set_ends(jax.random.randint(key_list[4], (N_POOL, N_DP, SPANS_DEV, NBR), 0, BLK_DEV), jax.random.fold_in(key_list[4], 1), 0, BLK_DEV - 1).astype(jnp.int32),
        "database": centred(key_list[5], (N_POOL, N_DP, BLK_DEV, NLEN, E), 1.0, 6.0, ((0, 4), (1, 32))),
        "lengths": draw_lengths(jax.random.fold_in(key_list[11], 71), 0),
        "gain": jnp.clip(1.0 + 0.15 * jax.random.normal(key_list[7], (E,), jnp.float32), 0.25, 1.75),
        "w_down": centred(key_list[8], (E, RANK), E ** -0.5, 0.25),
        "w_up": centred(key_list[9], (RANK, E), RANK ** -0.5, 0.375),
        "w_kv": centred(key_list[10], (E, 2 * HQ), E ** -0.5, 0.25),
    }


EPSILON = 1e-06
FLOOR = -1e+30

def encode_rows(block_rows, cond_rows, gain, w_down, w_up):
    x_full = block_rows.astype(jnp.float32) + cond_rows.astype(jnp.float32)[:, None, :]
    inv_rms = lax.rsqrt(lax.optimization_barrier(jnp.mean(x_full * x_full, axis=-1, keepdims=True)) + EPSILON)
    hidden = (x_full * inv_rms * gain).astype(jnp.bfloat16)
    flat_hidden = hidden.reshape(-1, hidden.shape[-1])
    latent = jnp.dot(flat_hidden, w_down, preferred_element_type=jnp.float32).astype(jnp.bfloat16)
    branch = jnp.dot(latent, w_up, preferred_element_type=jnp.float32).reshape(x_full.shape)
    encoded = (x_full + branch).astype(jnp.bfloat16)
    return (encoded, x_full, inv_rms, hidden, latent.reshape(x_full.shape[:-1] + (latent.shape[-1],)))

def encode_back(enc_grad, x_full, inv_rms, gain, w_down, w_up):
    flat_grad = enc_grad.reshape(-1, enc_grad.shape[-1])
    lat_grad = jnp.dot(flat_grad, w_up.T, preferred_element_type=jnp.float32).astype(jnp.bfloat16)
    hid_grad = jnp.dot(lat_grad, w_down.T, preferred_element_type=jnp.float32).reshape(x_full.shape)
    scaled = hid_grad * gain
    normed = x_full * inv_rms
    x_grad = enc_grad.astype(jnp.float32) + inv_rms * (scaled - normed * lax.optimization_barrier(jnp.mean(scaled * normed, axis=-1, keepdims=True)))
    return (lax.optimization_barrier(jnp.sum(x_grad, axis=-2)), lat_grad)

def attend(query_rows, cot_rows, encoded, block_len, w_kv):
    token_count = query_rows.shape[0]
    block_count = encoded.shape[0]
    span_count = token_count // SPAN
    key_count = NBR * NLEN
    scaling = HEAD ** (-0.5)
    key_value = jnp.dot(encoded.reshape(block_count * NLEN, E), w_kv, preferred_element_type=jnp.float32).astype(jnp.bfloat16)
    key_rows = key_value[:, :HQ].reshape(span_count, key_count, HEADS, HEAD).astype(jnp.float32)
    value_rows = key_value[:, HQ:].reshape(span_count, key_count, HEADS, HEAD).astype(jnp.float32)
    q_heads = query_rows.reshape(span_count, SPAN, HEADS, HEAD).astype(jnp.float32)
    out_grad = cot_rows.reshape(span_count, SPAN, HEADS, HEAD).astype(jnp.float32)
    usable = (jnp.arange(NLEN, dtype=jnp.int32)[None, :] < block_len[:, None]).reshape(span_count, 1, 1, key_count)
    scores = jnp.einsum('cqhd,ckhd->chqk', q_heads, key_rows) * scaling
    scores = jnp.where(usable, scores, FLOOR)
    row_max = lax.optimization_barrier(jnp.max(scores, axis=-1, keepdims=True))
    raised = jnp.exp(scores - row_max)
    probs = raised / lax.optimization_barrier(jnp.sum(raised, axis=-1, keepdims=True))
    probs_b = probs.astype(jnp.bfloat16).astype(jnp.float32)
    attn_out = jnp.einsum('chqk,ckhd->cqhd', probs_b, value_rows).astype(jnp.bfloat16).reshape(token_count, HQ)
    d_probs = jnp.einsum('cqhd,ckhd->chqk', out_grad, value_rows)
    delta = lax.optimization_barrier(jnp.sum(probs * d_probs, axis=-1, keepdims=True))
    d_scores = (probs * (d_probs - delta)).astype(jnp.bfloat16).astype(jnp.float32)
    q_grad = (jnp.einsum('chqk,ckhd->cqhd', d_scores, key_rows) * scaling).astype(jnp.bfloat16).reshape(token_count, HQ)
    key_grad = (jnp.einsum('chqk,cqhd->ckhd', d_scores, q_heads) * scaling).astype(jnp.bfloat16)
    value_grad = jnp.einsum('chqk,cqhd->ckhd', probs_b, out_grad).astype(jnp.bfloat16)
    kv_grad = jnp.concatenate([key_grad.reshape(block_count * NLEN, HQ), value_grad.reshape(block_count * NLEN, HQ)], axis=1)
    enc_grad = jnp.dot(kv_grad, w_kv.T, preferred_element_type=jnp.float32).astype(jnp.bfloat16)
    return (attn_out, q_grad, enc_grad.reshape(block_count, NLEN, E))

def reference(queries, cotangent, cond, nbr_owner, nbr_block, database, lengths, gain, w_down, w_up, w_kv):
    decoder_count = (N_POOL - 1) * N_DP
    store_rows = database[N_POOL - 1]
    store_len = lengths[N_POOL - 1]
    items = (queries[:N_POOL - 1].reshape(decoder_count, TOK_DEV, HQ), cotangent[:N_POOL - 1].reshape(decoder_count, TOK_DEV, HQ), cond[:N_POOL - 1].reshape(decoder_count, SPANS_DEV, E), nbr_owner[:N_POOL - 1].reshape(decoder_count, NB_DEV), nbr_block[:N_POOL - 1].reshape(decoder_count, NB_DEV))

    def one_device(carry, item):
        query_rows, cot_rows, cond_rows, owner_ids, block_ids = item
        block_rows = store_rows[owner_ids, block_ids]
        block_len = store_len[owner_ids, block_ids].astype(jnp.int32)
        cond_rep = jnp.repeat(cond_rows, NBR, axis=0)
        encoded, x_full, inv_rms, hidden, latent = encode_rows(block_rows, cond_rep, gain, w_down, w_up)
        attn_out, q_grad, enc_grad = attend(query_rows, cot_rows, encoded, block_len, w_kv)
        cond_rows_grad, lat_grad = encode_back(enc_grad, x_full, inv_rms, gain, w_down, w_up)
        down_term = jnp.dot(hidden.reshape(-1, E).T, lat_grad, preferred_element_type=jnp.float32)
        up_term = jnp.dot(enc_grad.reshape(-1, E).T, latent.reshape(-1, RANK), preferred_element_type=jnp.float32)
        span_grad = lax.optimization_barrier(jnp.sum(cond_rows_grad.reshape(SPANS_DEV, NBR, E), axis=1))
        return ((carry[0] + down_term, carry[1] + up_term), (attn_out, q_grad, span_grad))
    start = (jnp.zeros((E, RANK), jnp.float32), jnp.zeros((E, RANK), jnp.float32))
    sums, stacked = lax.scan(one_device, start, items)
    attn_all = jnp.concatenate([stacked[0].reshape(N_POOL - 1, N_DP, TOK_DEV, HQ), jnp.zeros((1, N_DP, TOK_DEV, HQ), jnp.bfloat16)], axis=0)
    qgrad_all = jnp.concatenate([stacked[1].reshape(N_POOL - 1, N_DP, TOK_DEV, HQ), jnp.zeros((1, N_DP, TOK_DEV, HQ), jnp.bfloat16)], axis=0)
    cgrad_all = jnp.concatenate([stacked[2].reshape(N_POOL - 1, N_DP, SPANS_DEV, E), jnp.zeros((1, N_DP, SPANS_DEV, E), jnp.float32)], axis=0)
    adapter_grad = jnp.concatenate([sums[0], sums[1]], axis=1)
    return (attn_all, qgrad_all, cgrad_all, adapter_grad)
```

```python
import jax
import jax.numpy as jnp
from jax import lax
from jax.sharding import PartitionSpec as P

HEADS = 16
HEAD = 128
SPAN = 64
EPSILON = 1e-06
FLOOR = -1e30


def encode_rows(block_rows, cond_rows, gain, w_down, w_up):
    x_full = block_rows.astype(jnp.float32) + cond_rows.astype(jnp.float32)[..., None, :]
    inv_rms = lax.rsqrt(jnp.mean(x_full * x_full, axis=-1, keepdims=True) + EPSILON)
    hidden = (x_full * inv_rms * gain).astype(jnp.bfloat16)
    flat_hidden = hidden.reshape(-1, hidden.shape[-1])
    latent = jnp.dot(flat_hidden, w_down, preferred_element_type=jnp.float32).astype(jnp.bfloat16)
    branch = jnp.dot(latent, w_up, preferred_element_type=jnp.float32).reshape(x_full.shape)
    encoded = (x_full + branch).astype(jnp.bfloat16)
    return encoded, x_full, inv_rms, flat_hidden, latent


def encode_back(enc_grad, x_full, inv_rms, gain, w_down, w_up):
    flat_grad = enc_grad.reshape(-1, enc_grad.shape[-1])
    lat_grad = jnp.dot(flat_grad, w_up.T, preferred_element_type=jnp.float32).astype(jnp.bfloat16)
    hid_grad = jnp.dot(lat_grad, w_down.T, preferred_element_type=jnp.float32).reshape(x_full.shape)
    scaled = hid_grad * gain
    normed = x_full * inv_rms
    x_grad = enc_grad.astype(jnp.float32) + inv_rms * (
        scaled - normed * jnp.mean(scaled * normed, axis=-1, keepdims=True)
    )
    return jnp.sum(x_grad, axis=-2), lat_grad


def attend(query_rows, cot_rows, encoded, block_len, w_kv):
    token_count, head_cols = query_rows.shape
    block_count, slot_len, enc_width = encoded.shape
    span_count = token_count // SPAN
    key_count = block_count * slot_len // span_count
    scaling = HEAD ** (-0.5)
    key_value = jnp.dot(
        encoded.reshape(block_count * slot_len, enc_width), w_kv, preferred_element_type=jnp.float32
    ).astype(jnp.bfloat16)
    key_rows = key_value[:, :head_cols].reshape(span_count, key_count, HEADS, HEAD)
    value_rows = key_value[:, head_cols:].reshape(span_count, key_count, HEADS, HEAD)
    q_heads = query_rows.reshape(span_count, SPAN, HEADS, HEAD)
    out_grad = cot_rows.reshape(span_count, SPAN, HEADS, HEAD)
    usable = (jnp.arange(slot_len, dtype=jnp.int32)[None, :] < block_len[:, None]).reshape(
        span_count, 1, 1, key_count
    )
    scores = (
        jnp.einsum("cqhd,ckhd->chqk", q_heads, key_rows, preferred_element_type=jnp.float32)
        * scaling
    )
    scores = jnp.where(usable, scores, FLOOR)
    row_max = jnp.max(scores, axis=-1, keepdims=True)
    raised = jnp.exp(scores - row_max)
    probs = raised / jnp.sum(raised, axis=-1, keepdims=True)
    probs_b = probs.astype(jnp.bfloat16)
    attn_out = (
        jnp.einsum("chqk,ckhd->cqhd", probs_b, value_rows, preferred_element_type=jnp.float32)
        .astype(jnp.bfloat16)
        .reshape(token_count, head_cols)
    )
    d_probs = jnp.einsum(
        "cqhd,ckhd->chqk", out_grad, value_rows, preferred_element_type=jnp.float32
    )
    delta = jnp.sum(probs * d_probs, axis=-1, keepdims=True)
    d_scores = (probs * (d_probs - delta)).astype(jnp.bfloat16)
    q_grad = (
        (
            jnp.einsum("chqk,ckhd->cqhd", d_scores, key_rows, preferred_element_type=jnp.float32)
            * scaling
        )
        .astype(jnp.bfloat16)
        .reshape(token_count, head_cols)
    )
    key_grad = (
        jnp.einsum("chqk,cqhd->ckhd", d_scores, q_heads, preferred_element_type=jnp.float32)
        * scaling
    ).astype(jnp.bfloat16)
    value_grad = jnp.einsum(
        "chqk,cqhd->ckhd", probs_b, out_grad, preferred_element_type=jnp.float32
    ).astype(jnp.bfloat16)
    kv_grad = jnp.concatenate(
        [
            key_grad.reshape(block_count * slot_len, head_cols),
            value_grad.reshape(block_count * slot_len, head_cols),
        ],
        axis=1,
    )
    enc_grad = lax.dot_general(
        kv_grad, w_kv, (((1,), (1,)), ((), ())), preferred_element_type=jnp.float32
    ).astype(jnp.bfloat16)
    return (attn_out, q_grad, enc_grad.reshape(block_count, slot_len, enc_width))


def body(
    queries, cotangent, cond, nbr_owner, nbr_block, database, lengths, gain, w_down, w_up, w_kv
):
    pools = lax.axis_size("pool")
    columns = lax.axis_size("dp")
    relay_row = pools - 1
    pool_index = lax.axis_index("pool")
    me = lax.axis_index("dp")
    on_encoder = pool_index == relay_row
    span_count = cond.shape[2]
    enc_width = cond.shape[3]
    nbr_count = nbr_owner.shape[3]
    per_device = span_count * nbr_count
    blk_dev = database.shape[2]
    slot_len = database.shape[3]
    token_count = queries.shape[2]
    head_cols = queries.shape[3]
    quarter = slot_len // pools

    meta = jnp.concatenate([nbr_owner.reshape(-1), nbr_block.reshape(-1), lengths.reshape(-1)])
    meta = lax.all_gather(meta, ("pool", "dp"), axis=0).reshape(pools, columns, -1)
    owner = jnp.swapaxes(meta[:relay_row, :, :per_device], 0, 1).reshape(columns, -1)
    block = jnp.swapaxes(meta[:relay_row, :, per_device : 2 * per_device], 0, 1).reshape(
        columns, -1
    )
    lens = meta[relay_row, :, 2 * per_device :]

    db4 = database.reshape(blk_dev, pools, quarter, enc_width)
    db4 = jnp.swapaxes(db4, 0, 1)
    mine = lax.all_to_all(db4, "pool", split_axis=0, concat_axis=0, tiled=True)[relay_row]

    live = owner.shape[1]
    order = jnp.arange(live, dtype=jnp.int32)[None, :]
    named = owner == me
    first = jnp.min(jnp.where(named, order, live), axis=1, keepdims=True)
    last = jnp.max(jnp.where(named, order, -1), axis=1, keepdims=True)
    b0 = jnp.sum(jnp.where(order == first, block, 0), axis=1)
    b1 = jnp.sum(jnp.where(order == last, block, 0), axis=1)
    slot_block = jnp.stack([b0, b1], axis=1).reshape(-1)
    send = jnp.take(mine, slot_block, axis=0).reshape(columns, 2, quarter, enc_width)

    got = lax.all_to_all(send, "dp", split_axis=0, concat_axis=0, tiled=True)
    got = got.reshape(columns * 2, quarter, enc_width)

    my_owner = lax.dynamic_index_in_dim(owner, me, 0, keepdims=False)
    my_block = lax.dynamic_index_in_dim(block, me, 0, keepdims=False)
    earlier = jnp.tril(jnp.ones((live, live), jnp.int32), -1)
    later = jnp.max(
        jnp.where(my_owner[:, None] == my_owner[None, :], earlier, 0), axis=1
    )
    position = my_owner * 2 + later
    pick = jnp.take(got, position, axis=0).reshape(relay_row, per_device, quarter, enc_width)
    pick = jnp.concatenate([pick, pick[:1]], axis=0)
    blocks = lax.all_to_all(pick, "pool", split_axis=0, concat_axis=0, tiled=True)
    blocks = jnp.swapaxes(blocks, 0, 1).reshape(per_device, slot_len, enc_width)

    own_row = jnp.minimum(pool_index, relay_row - 1)
    dec_owner = lax.dynamic_slice_in_dim(my_owner, own_row * per_device, per_device, 0)
    dec_block = lax.dynamic_slice_in_dim(my_block, own_row * per_device, per_device, 0)
    my_len = jnp.take(lens.reshape(-1), dec_owner * blk_dev + dec_block)

    def run(query_rows, cot_rows, blocks, my_len, cond_rows):
        cond_rep = jnp.repeat(cond_rows, nbr_count, axis=0)
        encoded, x_full, inv_rms, hidden, latent = encode_rows(
            blocks, cond_rep, gain, w_down, w_up
        )
        attn_out, q_grad, enc_grad = attend(query_rows, cot_rows, encoded, my_len, w_kv)
        cond_grad, lat_grad = encode_back(enc_grad, x_full, inv_rms, gain, w_down, w_up)
        flat_grad = enc_grad.reshape(-1, enc_width)
        down = lax.dot_general(
            hidden, lat_grad, (((0,), (0,)), ((), ())), preferred_element_type=jnp.float32
        )
        up = lax.dot_general(
            flat_grad, latent, (((0,), (0,)), ((), ())), preferred_element_type=jnp.float32
        )
        cond_grad = jnp.sum(cond_grad.reshape(span_count, nbr_count, enc_width), axis=1)
        return attn_out, q_grad, cond_grad, jnp.concatenate([down, up], axis=1)

    def skip(query_rows, cot_rows, blocks, my_len, cond_rows):
        return (
            jnp.zeros((token_count, head_cols), jnp.bfloat16),
            jnp.zeros((token_count, head_cols), jnp.bfloat16),
            jnp.zeros((span_count, enc_width), jnp.float32),
            jnp.zeros((enc_width, 2 * w_down.shape[1]), jnp.float32),
        )

    attn_out, q_grad, cond_grad, adapter = lax.cond(
        on_encoder,
        skip,
        run,
        queries.reshape(token_count, head_cols),
        cotangent.reshape(token_count, head_cols),
        blocks,
        my_len,
        cond.reshape(span_count, enc_width),
    )
    adapter_grad = lax.psum_scatter(
        adapter, ("pool", "dp"), scatter_dimension=0, tiled=True
    )
    return (
        attn_out.reshape(1, 1, token_count, head_cols),
        q_grad.reshape(1, 1, token_count, head_cols),
        cond_grad.reshape(1, 1, span_count, enc_width),
        adapter_grad,
    )


def solution(mesh):
    return jax.shard_map(
        body,
        mesh=mesh,
        in_specs=(
            P("pool", "dp", None, None),
            P("pool", "dp", None, None),
            P("pool", "dp", None, None),
            P("pool", "dp", None, None),
            P("pool", "dp", None, None),
            P("pool", "dp", None, None, None),
            P("pool", "dp", None),
            P(),
            P(),
            P(),
            P(),
        ),
        out_specs=(
            P("pool", "dp", None, None),
            P("pool", "dp", None, None),
            P("pool", "dp", None, None),
            P(("pool", "dp"), None),
        ),
        check_vma=False,
    )
```

```python
import functools
import jax
import jax.numpy as jnp
from jax import lax
from jax.experimental import pallas as pl
from jax.experimental.pallas import tpu as pltpu
from jax.sharding import PartitionSpec as P

HEAD = 128
SPAN = 64
EPSILON = 1e-06
FLOOR = -1e30
F32 = jnp.float32
BF16 = jnp.bfloat16


def dot_nn(a, b):
    return lax.dot_general(a, b, (((1,), (0,)), ((), ())), preferred_element_type=F32)


def dot_nt(a, b):
    return lax.dot_general(a, b, (((1,), (1,)), ((), ())), preferred_element_type=F32)


def dot_tn(a, b):
    return lax.dot_general(a, b, (((0,), (0,)), ((), ())), preferred_element_type=F32)


def attend_kernel(
    unroll, info, q_ref, do_ref, blk_ref, cond_ref, gain_ref, wd_ref, wu_ref, wkv_ref,
    out_ref, dq_ref, cg_ref, ad_ref, kv, kvg,
):
    c = pl.program_id(0)
    pools, nbr, quarter, width = blk_ref.shape
    slot_len = pools * quarter
    keys = nbr * slot_len
    hq = q_ref.shape[1]
    rank = wd_ref.shape[1]
    scaling = HEAD ** (-0.5)
    per_device = pl.num_programs(0) * nbr
    on_encoder = info[per_device] == 1

    @pl.when(c == 0)
    def _():
        ad_ref[...] = jnp.zeros_like(ad_ref)
        cg_ref[...] = jnp.zeros_like(cg_ref)

    @pl.when(on_encoder)
    def _():
        out_ref[...] = jnp.zeros_like(out_ref)
        dq_ref[...] = jnp.zeros_like(dq_ref)

    @pl.when(jnp.logical_not(on_encoder))
    def _():
        rows = jnp.concatenate(
            [blk_ref[p, n] for n in range(nbr) for p in range(pools)], axis=0
        ).astype(F32)
        cond = cond_ref[...].astype(F32)
        pick = lax.broadcasted_iota(jnp.int32, cond.shape, 0) == c
        cond_row = jnp.sum(jnp.where(pick, cond, 0.0), axis=0, keepdims=True)
        gain = gain_ref[...]
        x_full = rows + cond_row
        inv_rms = lax.rsqrt(jnp.mean(x_full * x_full, axis=-1, keepdims=True) + EPSILON)
        normed = x_full * inv_rms
        hidden = (normed * gain).astype(BF16)
        latent = dot_nn(hidden, wd_ref[...]).astype(BF16)
        encoded = (x_full + dot_nn(latent, wu_ref[...])).astype(BF16)
        for t in range(2 * hq // 512):
            cols = pl.ds(t * 512, 512)
            kv[:, cols] = dot_nn(encoded, wkv_ref[:, cols]).astype(BF16)

        slot = lax.broadcasted_iota(jnp.int32, (SPAN, keys), 1)
        bound = jnp.where(slot < slot_len, info[c * nbr], info[c * nbr + 1] + slot_len)
        usable = slot < bound

        def head(h):
            qs = pl.ds(pl.multiple_of(h * HEAD, HEAD), HEAD)
            vs = pl.ds(pl.multiple_of(hq + h * HEAD, HEAD), HEAD)
            q = q_ref[:, qs]
            do = do_ref[:, qs]
            k = kv[:, qs]
            v = kv[:, vs]
            s = jnp.where(usable, dot_nt(q, k) * scaling, FLOOR)
            dp = dot_nt(do, v)
            e = jnp.exp(s - jnp.max(s, axis=-1, keepdims=True))
            p = e * (1.0 / jnp.sum(e, axis=-1, keepdims=True))
            pb = p.astype(BF16)
            pdp = p * dp
            delta = jnp.sum(pdp, axis=-1, keepdims=True)
            ds = (pdp - p * delta).astype(BF16)
            out_ref[:, qs] = dot_nn(pb, v).astype(BF16)
            dq_ref[:, qs] = (dot_nn(ds, k) * scaling).astype(BF16)
            kvg[:, qs] = (dot_tn(ds, q) * scaling).astype(BF16)
            kvg[:, vs] = dot_tn(pb, do).astype(BF16)

        def heads(i, carry):
            for u in range(unroll):
                head(i * unroll + u)
            return carry

        lax.fori_loop(0, hq // HEAD // unroll, heads, 0)

        enc_grad = dot_nt(kvg[...], wkv_ref[...]).astype(BF16)
        lat_grad = dot_nt(enc_grad, wu_ref[...]).astype(BF16)
        scaled = dot_nt(lat_grad, wd_ref[...]) * gain
        mean = jnp.mean(scaled * normed, axis=-1, keepdims=True)
        x_grad = enc_grad.astype(F32) + inv_rms * (scaled - normed * mean)
        cg_ref[pl.ds(c, 1), :] = jnp.sum(x_grad, axis=0, keepdims=True)
        ad_ref[:, :rank] += dot_tn(hidden, lat_grad)
        ad_ref[:, rank:] += dot_tn(enc_grad, latent)


def attend(info, queries, cotangent, blocks, cond, gain, w_down, w_up, w_kv, unroll=2):
    tokens, hq = queries.shape
    pools, per_device, quarter, width = blocks.shape
    spans = cond.shape[0]
    nbr = per_device // spans
    rank = w_down.shape[1]
    whole = lambda shape: pl.BlockSpec(shape, lambda c, info: (0,) * len(shape))
    rows = pl.BlockSpec((SPAN, hq), lambda c, info: (c, 0))
    return pl.pallas_call(
        functools.partial(attend_kernel, unroll),
        out_shape=(
            jax.ShapeDtypeStruct((tokens, hq), BF16),
            jax.ShapeDtypeStruct((tokens, hq), BF16),
            jax.ShapeDtypeStruct((spans, width), F32),
            jax.ShapeDtypeStruct((width, 2 * rank), F32),
        ),
        grid_spec=pltpu.PrefetchScalarGridSpec(
            num_scalar_prefetch=1,
            grid=(spans,),
            in_specs=[
                rows,
                rows,
                pl.BlockSpec((pools, nbr, quarter, width), lambda c, info: (0, c, 0, 0)),
                whole((spans, width)),
                whole((1, width)),
                whole((width, rank)),
                whole((rank, width)),
                whole((width, 2 * hq)),
            ],
            out_specs=[rows, rows, whole((spans, width)), whole((width, 2 * rank))],
            scratch_shapes=[
                pltpu.VMEM((nbr * pools * quarter, 2 * hq), BF16),
                pltpu.VMEM((nbr * pools * quarter, 2 * hq), BF16),
            ],
        ),
        compiler_params=pltpu.CompilerParams(
            dimension_semantics=("arbitrary",), vmem_limit_bytes=56 << 20
        ),
        name="attend",
    )(info, queries, cotangent, blocks, cond, gain.reshape(1, width), w_down, w_up, w_kv)


def body(
    queries, cotangent, cond, nbr_owner, nbr_block, database, lengths, gain, w_down, w_up, w_kv
):
    pools = lax.axis_size("pool")
    columns = lax.axis_size("dp")
    relay_row = pools - 1
    pool_index = lax.axis_index("pool")
    me = lax.axis_index("dp")
    on_encoder = pool_index == relay_row
    span_count = cond.shape[2]
    enc_width = cond.shape[3]
    nbr_count = nbr_owner.shape[3]
    per_device = span_count * nbr_count
    blk_dev = database.shape[2]
    slot_len = database.shape[3]
    token_count = queries.shape[2]
    head_cols = queries.shape[3]
    quarter = slot_len // pools

    meta = jnp.concatenate([nbr_owner.reshape(-1), nbr_block.reshape(-1), lengths.reshape(-1)])
    meta = jnp.broadcast_to(meta[None], (pools * columns,) + meta.shape)
    meta = lax.all_to_all(meta, ("pool", "dp"), split_axis=0, concat_axis=0, tiled=True)
    meta = meta.reshape(pools, columns, -1)
    owner = jnp.swapaxes(meta[:relay_row, :, :per_device], 0, 1).reshape(columns, -1)
    block = jnp.swapaxes(meta[:relay_row, :, per_device : 2 * per_device], 0, 1).reshape(
        columns, -1
    )
    lens = meta[relay_row, :, 2 * per_device :]

    db4 = database.reshape(blk_dev, pools, quarter, enc_width)
    db4 = jnp.swapaxes(db4, 0, 1)
    mine = lax.all_to_all(db4, "pool", split_axis=0, concat_axis=0, tiled=True)[relay_row]

    live = owner.shape[1]
    order = jnp.arange(live, dtype=jnp.int32)[None, :]
    named = owner == me
    first = jnp.min(jnp.where(named, order, live), axis=1, keepdims=True)
    last = jnp.max(jnp.where(named, order, -1), axis=1, keepdims=True)
    b0 = jnp.sum(jnp.where(order == first, block, 0), axis=1)
    b1 = jnp.sum(jnp.where(order == last, block, 0), axis=1)
    slot_block = jnp.stack([b0, b1], axis=1).reshape(-1)
    send = jnp.take(mine, slot_block, axis=0).reshape(columns, 2, quarter, enc_width)

    got = lax.all_to_all(send, "dp", split_axis=0, concat_axis=0, tiled=True)
    got = got.reshape(columns * 2, quarter, enc_width)

    my_owner = lax.dynamic_index_in_dim(owner, me, 0, keepdims=False)
    my_block = lax.dynamic_index_in_dim(block, me, 0, keepdims=False)
    earlier = jnp.tril(jnp.ones((live, live), jnp.int32), -1)
    later = jnp.max(
        jnp.where(my_owner[:, None] == my_owner[None, :], earlier, 0), axis=1
    )
    position = my_owner * 2 + later
    pick = jnp.take(got, position, axis=0).reshape(relay_row, per_device, quarter, enc_width)
    pick = jnp.concatenate([pick, pick[:1]], axis=0)
    blocks = lax.all_to_all(pick, "pool", split_axis=0, concat_axis=0, tiled=True)

    own_row = jnp.minimum(pool_index, relay_row - 1)
    dec_owner = lax.dynamic_slice_in_dim(my_owner, own_row * per_device, per_device, 0)
    dec_block = lax.dynamic_slice_in_dim(my_block, own_row * per_device, per_device, 0)
    my_len = jnp.take(lens.reshape(-1), dec_owner * blk_dev + dec_block)

    info = jnp.concatenate([my_len, on_encoder.astype(jnp.int32)[None]])
    attn_out, q_grad, cond_grad, adapter = attend(
        info,
        queries.reshape(token_count, head_cols),
        cotangent.reshape(token_count, head_cols),
        blocks,
        cond.reshape(span_count, enc_width),
        gain,
        w_down,
        w_up,
        w_kv,
        unroll=4,
    )
    parts = pools * columns
    adapter = adapter.reshape(parts, enc_width // parts, -1)
    adapter = lax.all_to_all(adapter, ("pool", "dp"), split_axis=0, concat_axis=0, tiled=True)
    adapter_grad = jnp.sum(adapter, axis=0)
    return (
        attn_out.reshape(1, 1, token_count, head_cols),
        q_grad.reshape(1, 1, token_count, head_cols),
        cond_grad.reshape(1, 1, span_count, enc_width),
        adapter_grad,
    )


def solution(mesh):
    return jax.shard_map(
        body,
        mesh=mesh,
        in_specs=(
            P("pool", "dp", None, None),
            P("pool", "dp", None, None),
            P("pool", "dp", None, None),
            P("pool", "dp", None, None),
            P("pool", "dp", None, None),
            P("pool", "dp", None, None, None),
            P("pool", "dp", None),
            P(),
            P(),
            P(),
            P(),
        ),
        out_specs=(
            P("pool", "dp", None, None),
            P("pool", "dp", None, None),
            P("pool", "dp", None, None),
            P(("pool", "dp"), None),
        ),
        check_vma=False,
    )
```

```python
import functools
import jax
import jax.numpy as jnp
from jax import lax
from jax.experimental import pallas as pl
from jax.experimental.pallas import tpu as pltpu
from jax.sharding import PartitionSpec as P

HEAD = 128
SPAN = 64
EPSILON = 1e-06
FLOOR = -1e30
F32 = jnp.float32
BF16 = jnp.bfloat16


def dot_nn(a, b):
    return lax.dot_general(a, b, (((1,), (0,)), ((), ())), preferred_element_type=F32)


def dot_nt(a, b):
    return lax.dot_general(a, b, (((1,), (1,)), ((), ())), preferred_element_type=F32)


def dot_tn(a, b):
    return lax.dot_general(a, b, (((0,), (0,)), ((), ())), preferred_element_type=F32)


def attend_kernel(
    unroll, info, q_ref, do_ref, blk_ref, cond_ref, gain_ref, wd_ref, wu_ref, wkv_ref,
    out_ref, dq_ref, cg_ref, part_ref, kv, kvg, ad_ref,
):
    c = pl.program_id(0)
    pools, nbr, quarter, width = blk_ref.shape
    slot_len = pools * quarter
    keys = nbr * slot_len
    hq = q_ref.shape[1]
    rank = wd_ref.shape[1]
    scaling = HEAD ** (-0.5)
    per_device = pl.num_programs(0) * nbr
    on_encoder = info[per_device] == 1

    @pl.when(c == 0)
    def _():
        ad_ref[...] = jnp.zeros_like(ad_ref)
        cg_ref[...] = jnp.zeros_like(cg_ref)

    @pl.when(on_encoder)
    def _():
        out_ref[...] = jnp.zeros_like(out_ref)
        dq_ref[...] = jnp.zeros_like(dq_ref)

    @pl.when(jnp.logical_not(on_encoder))
    def _():
        rows = jnp.concatenate(
            [blk_ref[p, n] for n in range(nbr) for p in range(pools)], axis=0
        ).astype(F32)
        cond = cond_ref[...].astype(F32)
        pick = lax.broadcasted_iota(jnp.int32, cond.shape, 0) == c
        cond_row = jnp.sum(jnp.where(pick, cond, 0.0), axis=0, keepdims=True)
        gain = gain_ref[...]
        x_full = rows + cond_row
        inv_rms = lax.rsqrt(jnp.mean(x_full * x_full, axis=-1, keepdims=True) + EPSILON)
        normed = x_full * inv_rms
        hidden = (normed * gain).astype(BF16)
        latent = dot_nn(hidden, wd_ref[...]).astype(BF16)
        encoded = (x_full + dot_nn(latent, wu_ref[...])).astype(BF16)
        for t in range(2 * hq // 512):
            cols = pl.ds(t * 512, 512)
            kv[:, cols] = dot_nn(encoded, wkv_ref[:, cols]).astype(BF16)

        slot = lax.broadcasted_iota(jnp.int32, (SPAN, keys), 1)
        bound = jnp.where(slot < slot_len, info[c * nbr], info[c * nbr + 1] + slot_len)
        usable = slot < bound

        def head(h):
            qs = pl.ds(pl.multiple_of(h * HEAD, HEAD), HEAD)
            vs = pl.ds(pl.multiple_of(hq + h * HEAD, HEAD), HEAD)
            q = q_ref[:, qs]
            do = do_ref[:, qs]
            k = kv[:, qs]
            v = kv[:, vs]
            s = jnp.where(usable, dot_nt(q, k) * scaling, FLOOR)
            dp = dot_nt(do, v)
            e = jnp.exp(s - jnp.max(s, axis=-1, keepdims=True))
            p = e * (1.0 / jnp.sum(e, axis=-1, keepdims=True))
            pb = p.astype(BF16)
            pdp = p * dp
            delta = jnp.sum(pdp, axis=-1, keepdims=True)
            ds = (pdp - p * delta).astype(BF16)
            out_ref[:, qs] = dot_nn(pb, v).astype(BF16)
            dq_ref[:, qs] = (dot_nn(ds, k) * scaling).astype(BF16)
            kvg[:, qs] = (dot_tn(ds, q) * scaling).astype(BF16)
            kvg[:, vs] = dot_tn(pb, do).astype(BF16)

        def heads(i, carry):
            for u in range(unroll):
                head(i * unroll + u)
            return carry

        lax.fori_loop(0, hq // HEAD // unroll, heads, 0)

        enc_grad = dot_nt(kvg[...], wkv_ref[...]).astype(BF16)
        lat_grad = dot_nt(enc_grad, wu_ref[...]).astype(BF16)
        scaled = dot_nt(lat_grad, wd_ref[...]) * gain
        mean = jnp.mean(scaled * normed, axis=-1, keepdims=True)
        x_grad = enc_grad.astype(F32) + inv_rms * (scaled - normed * mean)
        cg_ref[pl.ds(c, 1), :] = jnp.sum(x_grad, axis=0, keepdims=True)
        ad_ref[:, :rank] += dot_tn(hidden, lat_grad)
        ad_ref[:, rank:] += dot_tn(enc_grad, latent)

    @pl.when(c == pl.num_programs(0) - 1)
    def _():
        columns, pools_out, piece, _ = part_ref.shape
        for p in range(pools_out):
            for j in range(columns):
                part_ref[j, p] = ad_ref[pl.ds((p * columns + j) * piece, piece), :]


def attend(columns, info, queries, cotangent, blocks, cond, gain, w_down, w_up, w_kv, unroll=2):
    tokens, hq = queries.shape
    pools, per_device, quarter, width = blocks.shape
    spans = cond.shape[0]
    nbr = per_device // spans
    rank = w_down.shape[1]
    whole = lambda shape: pl.BlockSpec(shape, lambda c, info: (0,) * len(shape))
    rows = pl.BlockSpec((SPAN, hq), lambda c, info: (c, 0))
    return pl.pallas_call(
        functools.partial(attend_kernel, unroll),
        out_shape=(
            jax.ShapeDtypeStruct((tokens, hq), BF16),
            jax.ShapeDtypeStruct((tokens, hq), BF16),
            jax.ShapeDtypeStruct((spans, width), F32),
            jax.ShapeDtypeStruct((columns, pools, width // (pools * columns), 2 * rank), F32),
        ),
        grid_spec=pltpu.PrefetchScalarGridSpec(
            num_scalar_prefetch=1,
            grid=(spans,),
            in_specs=[
                rows,
                rows,
                pl.BlockSpec((pools, nbr, quarter, width), lambda c, info: (0, c, 0, 0)),
                whole((spans, width)),
                whole((1, width)),
                whole((width, rank)),
                whole((rank, width)),
                whole((width, 2 * hq)),
            ],
            out_specs=[
                rows,
                rows,
                whole((spans, width)),
                whole((columns, pools, width // (pools * columns), 2 * rank)),
            ],
            scratch_shapes=[
                pltpu.VMEM((nbr * pools * quarter, 2 * hq), BF16),
                pltpu.VMEM((nbr * pools * quarter, 2 * hq), BF16),
                pltpu.VMEM((width, 2 * rank), F32),
            ],
        ),
        compiler_params=pltpu.CompilerParams(
            dimension_semantics=("arbitrary",), vmem_limit_bytes=56 << 20
        ),
        name="attend",
    )(info, queries, cotangent, blocks, cond, gain.reshape(1, width), w_down, w_up, w_kv)


MESH = pl.DeviceIdType.MESH


def greet(pools, columns):
    pool, me = lax.axis_index("pool"), lax.axis_index("dp")
    barrier = pltpu.get_barrier_semaphore()

    def hello(d, carry):
        pl.semaphore_signal(
            barrier, inc=1, device_id={"dp": lax.rem(me + d, columns)}, device_id_type=MESH
        )
        return carry

    lax.fori_loop(1, columns, hello, 0)
    for d in range(1, pools):
        pl.semaphore_signal(
            barrier, inc=1, device_id={"pool": lax.rem(pool + d, pools)}, device_id_type=MESH
        )
    pl.semaphore_wait(barrier, columns - 1 + pools - 1)


def fetch_kernel(
    pools, columns, owner_ref, block_ref, len_ref, db_ref, out_ref, info_ref,
    row, metas, smeta, table, place, share, send, got, pick,
    local_sem, base_send, base_recv, row_send, row_recv, meta_send, meta_recv,
    slot_send, slot_recv, pick_send, pick_recv,
):
    pool, me = lax.axis_index("pool"), lax.axis_index("dp")
    top = pools - 1
    spans, nbr = owner_ref.shape
    per = spans * nbr
    blocks, quarter = share.shape[0], share.shape[1]
    is_enc = pool == top
    greet(pools, columns)

    def base_copy(p):
        return pltpu.make_async_remote_copy(
            src_ref=db_ref.at[:, pl.ds(p * quarter, quarter), :],
            dst_ref=share,
            send_sem=base_send.at[p],
            recv_sem=base_recv,
            device_id={"pool": p},
            device_id_type=MESH,
        )

    base_own = pltpu.make_async_copy(
        db_ref.at[:, pl.ds(top * quarter, quarter), :], share, local_sem.at[0]
    )

    @pl.when(is_enc)
    def _():
        for p in range(top):
            base_copy(p).start()
        base_own.start()

    lane = lax.broadcasted_iota(jnp.int32, (1, 128), 1)
    line = jnp.zeros((1, 128), jnp.int32)
    for k in range(per):
        line = jnp.where(lane == k, owner_ref[k // nbr, k % nbr], line)
        line = jnp.where(lane == per + k, block_ref[k // nbr, k % nbr], line)
    for k in range(blocks):
        line = jnp.where(lane == 2 * per + k, len_ref[0, k], line)
    row[...] = line
    metas[me, pool] = line

    def row_copy(d):
        return pltpu.make_async_remote_copy(
            src_ref=row,
            dst_ref=metas.at[me, pool],
            send_sem=row_send.at[d],
            recv_sem=row_recv.at[pools - d],
            device_id={"pool": lax.rem(pool + d, pools)},
            device_id_type=MESH,
        )

    for d in range(1, pools):
        row_copy(d).start()
    for d in range(1, pools):
        row_copy(d).wait()

    def meta_copy(d):
        return pltpu.make_async_remote_copy(
            src_ref=metas.at[me],
            dst_ref=metas.at[me],
            send_sem=meta_send.at[d],
            recv_sem=meta_recv.at[columns - d],
            device_id={"dp": lax.rem(me + d, columns)},
            device_id_type=MESH,
        )

    def each(action):
        def step(d, carry):
            action(d)
            return carry

        lax.fori_loop(1, columns, step, 0)

    each(lambda d: meta_copy(d).start())
    each(lambda d: meta_copy(d).wait())
    to_scalar = pltpu.make_async_copy(metas, smeta, local_sem.at[1])
    to_scalar.start()
    to_scalar.wait()

    def find(j, carry):
        first, last = jnp.int32(0), jnp.int32(0)
        for q in range(top * per):
            p, k = q // per, q % per
            last = jnp.where(smeta[j, p, 0, k] == me, smeta[j, p, 0, per + k], last)
            p, k = (top * per - 1 - q) // per, (top * per - 1 - q) % per
            first = jnp.where(smeta[j, p, 0, k] == me, smeta[j, p, 0, per + k], first)
        table[2 * j] = first
        table[2 * j + 1] = last
        return carry

    lax.fori_loop(0, columns, find, 0)

    @pl.when(is_enc)
    def _():
        base_own.wait()
        for p in range(top):
            base_copy(p).wait_send()

    @pl.when(jnp.logical_not(is_enc))
    def _():
        base_copy(0).wait_recv()

    def fill(j, carry):
        for r in range(2):
            send[j, r] = share[table[2 * j + r]]
        return carry

    lax.fori_loop(0, columns, fill, 0)
    for r in range(2):
        got[2 * me + r] = share[table[2 * me + r]]

    def slot_copy(d):
        to = lax.rem(me + d, columns)
        return pltpu.make_async_remote_copy(
            src_ref=send.at[to],
            dst_ref=got.at[pl.ds(2 * me, 2)],
            send_sem=slot_send.at[d],
            recv_sem=slot_recv.at[columns - d],
            device_id={"dp": to},
            device_id_type=MESH,
        )

    each(lambda d: slot_copy(d).start())

    named = [smeta[me, q // per, 0, q % per] for q in range(top * per)]
    for q in range(top * per):
        again = jnp.int32(0)
        for e in range(q):
            again = jnp.where(named[e] == named[q], 1, again)
        place[q] = 2 * named[q] + again
    mine = jnp.minimum(pool, top - 1)
    for k in range(per):
        info_ref[k] = smeta[smeta[me, mine, 0, k], top, 0, 2 * per + smeta[me, mine, 0, per + k]]
    for k in range(per, info_ref.shape[0]):
        info_ref[k] = is_enc.astype(jnp.int32)

    each(lambda d: slot_copy(d).wait())

    def choose(q, carry):
        pick[q] = got[place[q]]
        return carry

    lax.fori_loop(0, top * per, choose, 0)

    def pick_copy(p):
        return pltpu.make_async_remote_copy(
            src_ref=pick.at[pl.ds(p * per, per)],
            dst_ref=out_ref.at[pool],
            send_sem=pick_send.at[p],
            recv_sem=pick_recv.at[pool],
            device_id={"pool": p},
            device_id_type=MESH,
        )

    def pick_from(p):
        return pltpu.make_async_remote_copy(
            src_ref=pick.at[pl.ds(0, per)],
            dst_ref=out_ref.at[p],
            send_sem=pick_send.at[p],
            recv_sem=pick_recv.at[p],
            device_id={"pool": p},
            device_id_type=MESH,
        )

    pick_own = pltpu.make_async_copy(
        pick.at[pl.ds(mine * per, per)], out_ref.at[pool], local_sem.at[2]
    )
    for p in range(top):

        @pl.when(pool != p)
        def _():
            pick_copy(p).start()

    pick_own.start()
    pick_own.wait()
    for p in range(top):

        @pl.when(pool != p)
        def _():
            pick_copy(p).wait_send()

    for p in range(pools):

        @pl.when(jnp.logical_and(pool != p, jnp.logical_not(is_enc)))
        def _():
            pick_from(p).wait_recv()


def fetch(pools, columns, nbr_owner, nbr_block, lengths, database):
    blocks, slot_len, width = database.shape
    per = nbr_owner.size
    quarter = slot_len // pools
    live = (pools - 1) * per
    dma = pltpu.SemaphoreType.DMA
    return pl.pallas_call(
        functools.partial(fetch_kernel, pools, columns),
        out_shape=(
            jax.ShapeDtypeStruct((pools, per, quarter, width), BF16),
            jax.ShapeDtypeStruct((2 * per,), jnp.int32),
        ),
        in_specs=[pl.BlockSpec(memory_space=pltpu.SMEM)] * 3
        + [pl.BlockSpec(memory_space=pl.ANY)],
        out_specs=(
            pl.BlockSpec(memory_space=pltpu.VMEM),
            pl.BlockSpec(memory_space=pltpu.SMEM),
        ),
        scratch_shapes=[
            pltpu.VMEM((1, 128), jnp.int32),
            pltpu.VMEM((columns, pools, 1, 128), jnp.int32),
            pltpu.SMEM((columns, pools, 1, 128), jnp.int32),
            pltpu.SMEM((2 * columns,), jnp.int32),
            pltpu.SMEM((live,), jnp.int32),
            pltpu.VMEM((blocks, quarter, width), BF16),
            pltpu.VMEM((columns, 2, quarter, width), BF16),
            pltpu.VMEM((2 * columns, quarter, width), BF16),
            pltpu.VMEM((live, quarter, width), BF16),
            dma((3,)),
            dma((pools,)),
            dma,
            dma((pools,)),
            dma((pools,)),
            dma((columns,)),
            dma((columns,)),
            dma((columns,)),
            dma((columns,)),
            dma((pools,)),
            dma((pools,)),
        ],
        compiler_params=pltpu.CompilerParams(
            collective_id=0, has_side_effects=True, vmem_limit_bytes=40 << 20
        ),
        name="fetch",
    )(nbr_owner, nbr_block, lengths, database)


def sum_kernel(
    pools, columns, part_ref, out_ref, lands, held, tops,
    a_send, a_recv, b_send, b_recv,
):
    pool, me = lax.axis_index("pool"), lax.axis_index("dp")
    top = pools - 1
    is_dec = pool != top
    greet(pools, columns)

    def each(action):
        def step(d, carry):
            action(d)
            return carry

        lax.fori_loop(1, columns, step, 0)

    def a_copy(d):
        to = lax.rem(me + d, columns)
        return pltpu.make_async_remote_copy(
            src_ref=part_ref.at[to],
            dst_ref=lands.at[me],
            send_sem=a_send.at[d],
            recv_sem=a_recv.at[columns - d],
            device_id={"dp": to},
            device_id_type=MESH,
        )

    def b_copy(p):
        return pltpu.make_async_remote_copy(
            src_ref=held.at[p],
            dst_ref=tops.at[pool],
            send_sem=b_send.at[p],
            recv_sem=b_recv.at[pool],
            device_id={"pool": p},
            device_id_type=MESH,
        )

    def b_from(p):
        return pltpu.make_async_remote_copy(
            src_ref=held.at[p],
            dst_ref=tops.at[p],
            send_sem=b_send.at[p],
            recv_sem=b_recv.at[p],
            device_id={"pool": p},
            device_id_type=MESH,
        )

    @pl.when(is_dec)
    def _():
        each(lambda d: a_copy(d).start())
        lands[me] = part_ref[me]
        each(lambda d: a_copy(d).wait())

        def add(j, total):
            return total + lands[j]

        held[...] = lax.fori_loop(1, columns, add, lands[0])
        for p in range(pools):

            @pl.when(pool != p)
            def _():
                b_copy(p).start()

            @pl.when(pool == p)
            def _():
                tops[p] = held[p]

        for p in range(pools):

            @pl.when(pool != p)
            def _():
                b_copy(p).wait_send()

    for p in range(top):

        @pl.when(pool != p)
        def _():
            b_from(p).wait_recv()

    total = tops[0]
    for p in range(1, top):
        total = total + tops[p]
    out_ref[...] = total


def sum_parts(pools, columns, parts):
    rows, width = parts.shape[2:]
    dma = pltpu.SemaphoreType.DMA
    return pl.pallas_call(
        functools.partial(sum_kernel, pools, columns),
        out_shape=jax.ShapeDtypeStruct((rows, width), F32),
        in_specs=[pl.BlockSpec(memory_space=pltpu.VMEM)],
        out_specs=pl.BlockSpec(memory_space=pltpu.VMEM),
        scratch_shapes=[
            pltpu.VMEM(parts.shape, F32),
            pltpu.VMEM((pools, rows, width), F32),
            pltpu.VMEM((pools, rows, width), F32),
            dma((columns,)),
            dma((columns,)),
            dma((pools,)),
            dma((pools,)),
        ],
        compiler_params=pltpu.CompilerParams(
            collective_id=1, has_side_effects=True, vmem_limit_bytes=24 << 20
        ),
        name="sum_parts",
    )(parts)


def body(
    queries, cotangent, cond, nbr_owner, nbr_block, database, lengths, gain, w_down, w_up, w_kv
):
    pools = lax.axis_size("pool")
    columns = lax.axis_size("dp")
    tokens, hq = queries.shape[2:]
    spans, width = cond.shape[2:]
    blocks, info = fetch(
        pools,
        columns,
        nbr_owner.reshape(nbr_owner.shape[2:]),
        nbr_block.reshape(nbr_block.shape[2:]),
        lengths.reshape(1, -1),
        database.reshape(database.shape[2:]),
    )
    attn_out, q_grad, cond_grad, parts = attend(
        columns,
        info,
        queries.reshape(tokens, hq),
        cotangent.reshape(tokens, hq),
        blocks,
        cond.reshape(spans, width),
        gain,
        w_down,
        w_up,
        w_kv,
        unroll=4,
    )
    adapter_grad = sum_parts(pools, columns, parts)
    return (
        attn_out.reshape(1, 1, tokens, hq),
        q_grad.reshape(1, 1, tokens, hq),
        cond_grad.reshape(1, 1, spans, width),
        adapter_grad,
    )


def solution(mesh):
    return jax.shard_map(
        body,
        mesh=mesh,
        in_specs=(
            P("pool", "dp", None, None),
            P("pool", "dp", None, None),
            P("pool", "dp", None, None),
            P("pool", "dp", None, None),
            P("pool", "dp", None, None),
            P("pool", "dp", None, None, None),
            P("pool", "dp", None),
            P(),
            P(),
            P(),
            P(),
        ),
        out_specs=(
            P("pool", "dp", None, None),
            P("pool", "dp", None, None),
            P("pool", "dp", None, None),
            P(("pool", "dp"), None),
        ),
        check_vma=False,
    )
```

```python
import functools
import jax
import jax.numpy as jnp
from jax import lax
from jax.experimental import pallas as pl
from jax.experimental.pallas import tpu as pltpu
from jax.sharding import PartitionSpec as P

HEAD = 128
SPAN = 64
EPSILON = 1e-06
FLOOR = -1e30
F32 = jnp.float32
BF16 = jnp.bfloat16


def dot_nn(a, b):
    return lax.dot_general(a, b, (((1,), (0,)), ((), ())), preferred_element_type=F32)


def dot_nt(a, b):
    return lax.dot_general(a, b, (((1,), (1,)), ((), ())), preferred_element_type=F32)


def dot_tn(a, b):
    return lax.dot_general(a, b, (((0,), (0,)), ((), ())), preferred_element_type=F32)


def attend_kernel(
    unroll, info, q_ref, do_ref, blk_ref, cond_ref, gain_ref, wd_ref, wu_ref, wkv_ref,
    out_ref, dq_ref, cg_ref, part_ref, kv, kvg, ad_ref,
):
    c = pl.program_id(0)
    pools, nbr, quarter, width = blk_ref.shape
    slot_len = pools * quarter
    keys = nbr * slot_len
    hq = q_ref.shape[1]
    rank = wd_ref.shape[1]
    scaling = HEAD ** (-0.5)
    per_device = pl.num_programs(0) * nbr
    on_encoder = info[per_device] == 1

    @pl.when(c == 0)
    def _():
        ad_ref[...] = jnp.zeros_like(ad_ref)
        cg_ref[...] = jnp.zeros_like(cg_ref)

    @pl.when(on_encoder)
    def _():
        out_ref[...] = jnp.zeros_like(out_ref)
        dq_ref[...] = jnp.zeros_like(dq_ref)

    @pl.when(jnp.logical_not(on_encoder))
    def _():
        rows = jnp.concatenate(
            [blk_ref[p, n] for n in range(nbr) for p in range(pools)], axis=0
        ).astype(F32)
        cond = cond_ref[...].astype(F32)
        pick = lax.broadcasted_iota(jnp.int32, cond.shape, 0) == c
        cond_row = jnp.sum(jnp.where(pick, cond, 0.0), axis=0, keepdims=True)
        gain = gain_ref[...]
        x_full = rows + cond_row
        inv_rms = lax.rsqrt(jnp.mean(x_full * x_full, axis=-1, keepdims=True) + EPSILON)
        normed = x_full * inv_rms
        hidden = (normed * gain).astype(BF16)
        latent = dot_nn(hidden, wd_ref[...]).astype(BF16)
        encoded = (x_full + dot_nn(latent, wu_ref[...])).astype(BF16)
        for t in range(2 * hq // 512):
            cols = pl.ds(t * 512, 512)
            kv[:, cols] = dot_nn(encoded, wkv_ref[:, cols]).astype(BF16)

        slot = lax.broadcasted_iota(jnp.int32, (SPAN, keys), 1)
        bound = jnp.where(slot < slot_len, info[c * nbr], info[c * nbr + 1] + slot_len)
        usable = slot < bound

        def score(h):
            qs = pl.ds(h * HEAD, HEAD)
            vs = pl.ds(hq + h * HEAD, HEAD)
            s = dot_nt(q_ref[:, qs], kv[:, qs])
            dp = dot_nt(do_ref[:, qs], kv[:, vs])
            return s, dp

        def weigh(s, dp):
            s = jnp.where(usable, s * scaling, FLOOR)
            e = jnp.exp(s - jnp.max(s, axis=-1, keepdims=True))
            p = e * (1.0 / jnp.sum(e, axis=-1, keepdims=True))
            pdp = p * dp
            delta = jnp.sum(pdp, axis=-1, keepdims=True)
            return p.astype(BF16), (pdp - p * delta).astype(BF16)

        def finish(h, pb, ds):
            qs = pl.ds(h * HEAD, HEAD)
            vs = pl.ds(hq + h * HEAD, HEAD)
            out_ref[:, qs] = dot_nn(pb, kv[:, vs]).astype(BF16)
            dq_ref[:, qs] = (dot_nn(ds, kv[:, qs]) * scaling).astype(BF16)
            kvg[:, qs] = (dot_tn(ds, q_ref[:, qs]) * scaling).astype(BF16)
            kvg[:, vs] = dot_tn(pb, do_ref[:, qs]).astype(BF16)

        heads = hq // HEAD
        first, second = {}, {}
        for i in range(heads + 2 * unroll):
            if i < heads:
                first[i] = score(i)
            if 0 <= i - unroll < heads:
                second[i - unroll] = weigh(*first.pop(i - unroll))
            if 0 <= i - 2 * unroll < heads:
                finish(i - 2 * unroll, *second.pop(i - 2 * unroll))

        enc_grad = dot_nt(kvg[...], wkv_ref[...]).astype(BF16)
        lat_grad = dot_nt(enc_grad, wu_ref[...]).astype(BF16)
        scaled = dot_nt(lat_grad, wd_ref[...]) * gain
        mean = jnp.mean(scaled * normed, axis=-1, keepdims=True)
        x_grad = enc_grad.astype(F32) + inv_rms * (scaled - normed * mean)
        cg_ref[pl.ds(c, 1), :] = jnp.sum(x_grad, axis=0, keepdims=True)
        ad_ref[:, :rank] += dot_tn(hidden, lat_grad)
        ad_ref[:, rank:] += dot_tn(enc_grad, latent)

    @pl.when(c == pl.num_programs(0) - 1)
    def _():
        columns, pools_out, piece, _ = part_ref.shape
        for p in range(pools_out):
            for j in range(columns):
                part_ref[j, p] = ad_ref[pl.ds((p * columns + j) * piece, piece), :].astype(BF16)


def attend(columns, info, queries, cotangent, blocks, cond, gain, w_down, w_up, w_kv, unroll=2):
    tokens, hq = queries.shape
    pools, per_device, quarter, width = blocks.shape
    spans = cond.shape[0]
    nbr = per_device // spans
    rank = w_down.shape[1]
    whole = lambda shape: pl.BlockSpec(shape, lambda c, info: (0,) * len(shape))
    rows = pl.BlockSpec((SPAN, hq), lambda c, info: (c, 0))
    return pl.pallas_call(
        functools.partial(attend_kernel, unroll),
        out_shape=(
            jax.ShapeDtypeStruct((tokens, hq), BF16),
            jax.ShapeDtypeStruct((tokens, hq), BF16),
            jax.ShapeDtypeStruct((spans, width), F32),
            jax.ShapeDtypeStruct((columns, pools, width // (pools * columns), 2 * rank), BF16),
        ),
        grid_spec=pltpu.PrefetchScalarGridSpec(
            num_scalar_prefetch=1,
            grid=(spans,),
            in_specs=[
                rows,
                rows,
                pl.BlockSpec((pools, nbr, quarter, width), lambda c, info: (0, c, 0, 0)),
                whole((spans, width)),
                whole((1, width)),
                whole((width, rank)),
                whole((rank, width)),
                whole((width, 2 * hq)),
            ],
            out_specs=[
                rows,
                rows,
                whole((spans, width)),
                whole((columns, pools, width // (pools * columns), 2 * rank)),
            ],
            scratch_shapes=[
                pltpu.VMEM((nbr * pools * quarter, 2 * hq), BF16),
                pltpu.VMEM((nbr * pools * quarter, 2 * hq), BF16),
                pltpu.VMEM((width, 2 * rank), F32),
            ],
        ),
        compiler_params=pltpu.CompilerParams(
            dimension_semantics=("arbitrary",), vmem_limit_bytes=56 << 20
        ),
        name="attend",
    )(info, queries, cotangent, blocks, cond, gain.reshape(1, width), w_down, w_up, w_kv)


MESH = pl.DeviceIdType.MESH


def greet(pools, columns):
    pool, me = lax.axis_index("pool"), lax.axis_index("dp")
    barrier = pltpu.get_barrier_semaphore()

    def hello(d, carry):
        pl.semaphore_signal(
            barrier, inc=1, device_id={"dp": lax.rem(me + d, columns)}, device_id_type=MESH
        )
        return carry

    lax.fori_loop(1, columns, hello, 0)
    for d in range(1, pools):
        pl.semaphore_signal(
            barrier, inc=1, device_id={"pool": lax.rem(pool + d, pools)}, device_id_type=MESH
        )
    pl.semaphore_wait(barrier, columns - 1 + pools - 1)


def fetch_kernel(
    pools, columns, owner_ref, block_ref, len_ref, db_ref, out_ref, info_ref,
    row, metas, smeta, found, table, place, share, send, got, pick,
    local_sem, base_send, base_recv, row_send, row_recv, meta_send, meta_recv,
    slot_send, slot_recv, pick_send, pick_recv,
):
    pool, me = lax.axis_index("pool"), lax.axis_index("dp")
    top = pools - 1
    spans, nbr = owner_ref.shape
    per = spans * nbr
    blocks, quarter = share.shape[0], share.shape[1]
    is_enc = pool == top
    greet(pools, columns)

    def base_copy(p):
        return pltpu.make_async_remote_copy(
            src_ref=db_ref.at[:, pl.ds(p * quarter, quarter), :],
            dst_ref=share,
            send_sem=base_send.at[p],
            recv_sem=base_recv,
            device_id={"pool": p},
            device_id_type=MESH,
        )

    base_own = pltpu.make_async_copy(
        db_ref.at[:, pl.ds(top * quarter, quarter), :], share, local_sem.at[0]
    )

    lane = lax.broadcasted_iota(jnp.int32, (1, 128), 1)
    line = jnp.zeros((1, 128), jnp.int32)
    for k in range(per):
        line = jnp.where(lane == k, owner_ref[k // nbr, k % nbr], line)
        line = jnp.where(lane == per + k, block_ref[k // nbr, k % nbr], line)
    for k in range(blocks):
        line = jnp.where(lane == 2 * per + k, len_ref[0, k], line)
    row[...] = line
    metas[me, pool] = line

    def row_copy(d):
        return pltpu.make_async_remote_copy(
            src_ref=row,
            dst_ref=metas.at[me, pool],
            send_sem=row_send.at[d],
            recv_sem=row_recv.at[pools - d],
            device_id={"pool": lax.rem(pool + d, pools)},
            device_id_type=MESH,
        )

    for d in range(1, pools):
        row_copy(d).start()
    for d in range(1, pools):
        row_copy(d).wait()

    def meta_copy(d):
        return pltpu.make_async_remote_copy(
            src_ref=metas.at[me],
            dst_ref=metas.at[me],
            send_sem=meta_send.at[d],
            recv_sem=meta_recv.at[columns - d],
            device_id={"dp": lax.rem(me + d, columns)},
            device_id_type=MESH,
        )

    def each(action):
        def step(d, carry):
            action(d)
            return carry

        lax.fori_loop(1, columns, step, 0)

    each(lambda d: meta_copy(d).start())

    @pl.when(is_enc)
    def _():
        for p in range(top):
            base_copy(p).start()
        base_own.start()

    each(lambda d: meta_copy(d).wait())
    to_scalar = pltpu.make_async_copy(metas, smeta, local_sem.at[1])
    to_scalar.start()

    lanes = lax.broadcasted_iota(jnp.int32, (columns, 128), 1)
    least = jnp.full((columns, 128), blocks << 16, jnp.int32)
    most = jnp.zeros((columns, 128), jnp.int32)
    for p in range(top):
        lists = metas[:, p, 0, :]
        key = (lanes + (p * per + 1)) * blocks + pltpu.roll(lists, 128 - per, 1)
        named = jnp.logical_and(lists == me, lanes < per)
        least = jnp.minimum(least, jnp.where(named, key, blocks << 16))
        most = jnp.maximum(most, jnp.where(named, key, 0))
    least = jnp.bitwise_and(jnp.min(least, axis=1, keepdims=True), blocks - 1)
    most = jnp.bitwise_and(jnp.max(most, axis=1, keepdims=True), blocks - 1)
    found[...] = jnp.where(lanes == 0, least, most)
    to_table = pltpu.make_async_copy(found, table, local_sem.at[2])
    to_table.start()
    to_table.wait()

    @pl.when(is_enc)
    def _():
        base_own.wait()
        for p in range(top):
            base_copy(p).wait_send()

    @pl.when(jnp.logical_not(is_enc))
    def _():
        base_copy(0).wait_recv()

    def fill(j, carry):
        for r in range(2):
            send[j, r] = share[table[j, r]]
        return carry

    lax.fori_loop(0, columns, fill, 0)
    for r in range(2):
        got[2 * me + r] = share[table[me, r]]

    def slot_copy(d):
        to = lax.rem(me + d, columns)
        return pltpu.make_async_remote_copy(
            src_ref=send.at[to],
            dst_ref=got.at[pl.ds(2 * me, 2)],
            send_sem=slot_send.at[d],
            recv_sem=slot_recv.at[columns - d],
            device_id={"dp": to},
            device_id_type=MESH,
        )

    each(lambda d: slot_copy(d).start())

    to_scalar.wait()
    named = [smeta[me, q // per, 0, q % per] for q in range(top * per)]
    for q in range(top * per):
        again = jnp.int32(0)
        for e in range(q):
            again = jnp.where(named[e] == named[q], 1, again)
        place[q] = 2 * named[q] + again
    mine = jnp.minimum(pool, top - 1)
    for k in range(per):
        info_ref[k] = smeta[smeta[me, mine, 0, k], top, 0, 2 * per + smeta[me, mine, 0, per + k]]
    for k in range(per, info_ref.shape[0]):
        info_ref[k] = is_enc.astype(jnp.int32)

    each(lambda d: slot_copy(d).wait())

    def choose(q, carry):
        pick[q] = got[place[q]]
        return carry

    lax.fori_loop(0, top * per, choose, 0)

    def pick_copy(p):
        return pltpu.make_async_remote_copy(
            src_ref=pick.at[pl.ds(p * per, per)],
            dst_ref=out_ref.at[pool],
            send_sem=pick_send.at[p],
            recv_sem=pick_recv.at[pool],
            device_id={"pool": p},
            device_id_type=MESH,
        )

    def pick_from(p):
        return pltpu.make_async_remote_copy(
            src_ref=pick.at[pl.ds(0, per)],
            dst_ref=out_ref.at[p],
            send_sem=pick_send.at[p],
            recv_sem=pick_recv.at[p],
            device_id={"pool": p},
            device_id_type=MESH,
        )

    pick_own = pltpu.make_async_copy(
        pick.at[pl.ds(mine * per, per)], out_ref.at[pool], local_sem.at[3]
    )
    for p in range(top):

        @pl.when(pool != p)
        def _():
            pick_copy(p).start()

    pick_own.start()
    pick_own.wait()
    for p in range(top):

        @pl.when(pool != p)
        def _():
            pick_copy(p).wait_send()

    for p in range(pools):

        @pl.when(jnp.logical_and(pool != p, jnp.logical_not(is_enc)))
        def _():
            pick_from(p).wait_recv()


def fetch(pools, columns, nbr_owner, nbr_block, lengths, database):
    blocks, slot_len, width = database.shape
    per = nbr_owner.size
    quarter = slot_len // pools
    live = (pools - 1) * per
    dma = pltpu.SemaphoreType.DMA
    return pl.pallas_call(
        functools.partial(fetch_kernel, pools, columns),
        out_shape=(
            jax.ShapeDtypeStruct((pools, per, quarter, width), BF16),
            jax.ShapeDtypeStruct((2 * per,), jnp.int32),
        ),
        in_specs=[pl.BlockSpec(memory_space=pltpu.SMEM)] * 3
        + [pl.BlockSpec(memory_space=pl.ANY)],
        out_specs=(
            pl.BlockSpec(memory_space=pltpu.VMEM),
            pl.BlockSpec(memory_space=pltpu.SMEM),
        ),
        scratch_shapes=[
            pltpu.VMEM((1, 128), jnp.int32),
            pltpu.VMEM((columns, pools, 1, 128), jnp.int32),
            pltpu.SMEM((columns, pools, 1, 128), jnp.int32),
            pltpu.VMEM((columns, 128), jnp.int32),
            pltpu.SMEM((columns, 128), jnp.int32),
            pltpu.SMEM((live,), jnp.int32),
            pltpu.VMEM((blocks, quarter, width), BF16),
            pltpu.VMEM((columns, 2, quarter, width), BF16),
            pltpu.VMEM((2 * columns, quarter, width), BF16),
            pltpu.VMEM((live, quarter, width), BF16),
            dma((4,)),
            dma((pools,)),
            dma,
            dma((pools,)),
            dma((pools,)),
            dma((columns,)),
            dma((columns,)),
            dma((columns,)),
            dma((columns,)),
            dma((pools,)),
            dma((pools,)),
        ],
        compiler_params=pltpu.CompilerParams(
            collective_id=0, has_side_effects=True, vmem_limit_bytes=40 << 20
        ),
        name="fetch",
    )(nbr_owner, nbr_block, lengths, database)


def sum_kernel(
    pools, columns, part_ref, out_ref, lands, held, tops,
    a_send, a_recv, b_send, b_recv,
):
    pool, me = lax.axis_index("pool"), lax.axis_index("dp")
    top = pools - 1
    is_dec = pool != top
    greet(pools, columns)

    def each(action):
        def step(d, carry):
            action(d)
            return carry

        lax.fori_loop(1, columns, step, 0)

    def a_copy(d):
        to = lax.rem(me + d, columns)
        return pltpu.make_async_remote_copy(
            src_ref=part_ref.at[to],
            dst_ref=lands.at[me],
            send_sem=a_send.at[d],
            recv_sem=a_recv.at[columns - d],
            device_id={"dp": to},
            device_id_type=MESH,
        )

    def b_copy(p):
        return pltpu.make_async_remote_copy(
            src_ref=held.at[p],
            dst_ref=tops.at[pool],
            send_sem=b_send.at[p],
            recv_sem=b_recv.at[pool],
            device_id={"pool": p},
            device_id_type=MESH,
        )

    def b_from(p):
        return pltpu.make_async_remote_copy(
            src_ref=held.at[p],
            dst_ref=tops.at[p],
            send_sem=b_send.at[p],
            recv_sem=b_recv.at[p],
            device_id={"pool": p},
            device_id_type=MESH,
        )

    @pl.when(is_dec)
    def _():
        each(lambda d: a_copy(d).start())
        lands[me] = part_ref[me]
        each(lambda d: a_copy(d).wait())

        def add(j, total):
            return total + lands[j].astype(F32)

        held[...] = lax.fori_loop(1, columns, add, lands[0].astype(F32))
        for p in range(pools):

            @pl.when(pool != p)
            def _():
                b_copy(p).start()

            @pl.when(pool == p)
            def _():
                tops[p] = held[p]

        for p in range(pools):

            @pl.when(pool != p)
            def _():
                b_copy(p).wait_send()

    for p in range(top):

        @pl.when(pool != p)
        def _():
            b_from(p).wait_recv()

    total = tops[0]
    for p in range(1, top):
        total = total + tops[p]
    out_ref[...] = total


def sum_parts(pools, columns, parts):
    rows, width = parts.shape[2:]
    dma = pltpu.SemaphoreType.DMA
    return pl.pallas_call(
        functools.partial(sum_kernel, pools, columns),
        out_shape=jax.ShapeDtypeStruct((rows, width), F32),
        in_specs=[pl.BlockSpec(memory_space=pltpu.VMEM)],
        out_specs=pl.BlockSpec(memory_space=pltpu.VMEM),
        scratch_shapes=[
            pltpu.VMEM(parts.shape, BF16),
            pltpu.VMEM((pools, rows, width), F32),
            pltpu.VMEM((pools, rows, width), F32),
            dma((columns,)),
            dma((columns,)),
            dma((pools,)),
            dma((pools,)),
        ],
        compiler_params=pltpu.CompilerParams(
            collective_id=1, has_side_effects=True, vmem_limit_bytes=24 << 20
        ),
        name="sum_parts",
    )(parts)


def body(
    queries, cotangent, cond, nbr_owner, nbr_block, database, lengths, gain, w_down, w_up, w_kv
):
    pools = lax.axis_size("pool")
    columns = lax.axis_size("dp")
    tokens, hq = queries.shape[2:]
    spans, width = cond.shape[2:]
    blocks, info = fetch(
        pools,
        columns,
        nbr_owner.reshape(nbr_owner.shape[2:]),
        nbr_block.reshape(nbr_block.shape[2:]),
        lengths.reshape(1, -1),
        database.reshape(database.shape[2:]),
    )
    attn_out, q_grad, cond_grad, parts = attend(
        columns,
        info,
        queries.reshape(tokens, hq),
        cotangent.reshape(tokens, hq),
        blocks,
        cond.reshape(spans, width),
        gain,
        w_down,
        w_up,
        w_kv,
        unroll=4,
    )
    adapter_grad = sum_parts(pools, columns, parts)
    return (
        attn_out.reshape(1, 1, tokens, hq),
        q_grad.reshape(1, 1, tokens, hq),
        cond_grad.reshape(1, 1, spans, width),
        adapter_grad,
    )


def solution(mesh):
    return jax.shard_map(
        body,
        mesh=mesh,
        in_specs=(
            P("pool", "dp", None, None),
            P("pool", "dp", None, None),
            P("pool", "dp", None, None),
            P("pool", "dp", None, None),
            P("pool", "dp", None, None),
            P("pool", "dp", None, None, None),
            P("pool", "dp", None),
            P(),
            P(),
            P(),
            P(),
        ),
        out_specs=(
            P("pool", "dp", None, None),
            P("pool", "dp", None, None),
            P("pool", "dp", None, None),
            P(("pool", "dp"), None),
        ),
        check_vma=False,
    )
```

```python
import functools

import jax
import jax.numpy as jnp
from jax import lax
from jax.experimental import pallas as pl
from jax.experimental.pallas import tpu as pltpu
from jax.sharding import PartitionSpec as P

HEAD = 128
SPAN = 64
EPSILON = 1e-06
FLOOR = -1e30
STAGE = 4
F32 = jnp.float32
BF16 = jnp.bfloat16
MESH = pl.DeviceIdType.MESH


def dot_nn(a, b):
    return lax.dot_general(a, b, (((1,), (0,)), ((), ())), preferred_element_type=F32)


def dot_nt(a, b):
    return lax.dot_general(a, b, (((1,), (1,)), ((), ())), preferred_element_type=F32)


def dot_tn(a, b):
    return lax.dot_general(a, b, (((0,), (0,)), ((), ())), preferred_element_type=F32)


def greet(pools, columns):
    pool, me = lax.axis_index("pool"), lax.axis_index("dp")
    barrier = pltpu.get_barrier_semaphore()

    def hello(d, carry):
        pl.semaphore_signal(
            barrier, inc=1, device_id={"dp": lax.rem(me + d, columns)}, device_id_type=MESH
        )
        return carry

    lax.fori_loop(1, columns, hello, 0)
    for d in range(1, pools):
        pl.semaphore_signal(
            barrier, inc=1, device_id={"pool": lax.rem(pool + d, pools)}, device_id_type=MESH
        )
    pl.semaphore_wait(barrier, columns - 1 + pools - 1)


def whole_kernel(
    pools, columns,
    owner_ref, block_ref, len_ref, db_ref, q_hbm, do_hbm, cond_ref, gain_ref, wd_hbm, wu_hbm,
    wkv_hbm,
    out_ref, dq_ref, cg_ref, sum_ref,
    row, metas, smeta, found, table, place, lens, share, send, got, pick, blk,
    q_ref, do_ref, wd_ref, wu_ref, wkv_ref, kv, kvg, ad_ref, part, lands, held, tops,
    load_sem, local_sem, base_send, base_recv, row_send, row_recv, meta_send, meta_recv,
    slot_send, slot_recv, pick_send, pick_recv, a_send, a_recv, b_send, b_recv,
):
    pool, me = lax.axis_index("pool"), lax.axis_index("dp")
    top = pools - 1
    nbr, spans = owner_ref.shape
    per = spans * nbr
    blocks, quarter, width = share.shape
    hq = q_ref.shape[1]
    rank = wd_ref.shape[1]
    slot_len = pools * quarter
    is_enc = pool == top
    is_dec = jnp.logical_not(is_enc)

    loads = [
        pltpu.make_async_copy(a, b, load_sem.at[i])
        for i, (a, b) in enumerate(
            ((wd_hbm, wd_ref), (wu_hbm, wu_ref), (wkv_hbm, wkv_ref), (q_hbm, q_ref), (do_hbm, do_ref))
        )
    ]

    @pl.when(is_dec)
    def _():
        for load in loads:
            load.start()

    def each(action):
        def step(d, carry):
            action(d)
            return carry

        lax.fori_loop(1, columns, step, 0)

    lane = lax.broadcasted_iota(jnp.int32, (1, 128), 1)
    line = jnp.zeros((1, 128), jnp.int32)
    for k in range(per):
        line = jnp.where(lane == k, owner_ref[k % nbr, k // nbr], line)
        line = jnp.where(lane == per + k, block_ref[k % nbr, k // nbr], line)
    for k in range(blocks):
        line = jnp.where(lane == 2 * per + k, len_ref[0, k], line)
    row[...] = line
    metas[me, pool] = line
    greet(pools, columns)

    def row_copy(d):
        return pltpu.make_async_remote_copy(
            src_ref=row,
            dst_ref=metas.at[me, pool],
            send_sem=row_send.at[d],
            recv_sem=row_recv.at[pools - d],
            device_id={"pool": lax.rem(pool + d, pools)},
            device_id_type=MESH,
        )

    for d in range(1, pools):
        row_copy(d).start()
    for d in range(1, pools):
        row_copy(d).wait()

    def meta_copy(d):
        return pltpu.make_async_remote_copy(
            src_ref=metas.at[me],
            dst_ref=metas.at[me],
            send_sem=meta_send.at[d],
            recv_sem=meta_recv.at[columns - d],
            device_id={"dp": lax.rem(me + d, columns)},
            device_id_type=MESH,
        )

    each(lambda d: meta_copy(d).start())

    def base_copy(p):
        return pltpu.make_async_remote_copy(
            src_ref=db_ref.at[:, pl.ds(p * quarter, quarter), :],
            dst_ref=share,
            send_sem=base_send.at[p],
            recv_sem=base_recv,
            device_id={"pool": p},
            device_id_type=MESH,
        )

    base_own = pltpu.make_async_copy(
        db_ref.at[:, pl.ds(top * quarter, quarter), :], share, local_sem.at[0]
    )

    @pl.when(is_enc)
    def _():
        for p in range(top):
            base_copy(p).start()
        base_own.start()

    each(lambda d: meta_copy(d).wait())
    to_scalar = pltpu.make_async_copy(metas, smeta, local_sem.at[1])
    to_scalar.start()

    lanes = lax.broadcasted_iota(jnp.int32, (columns, 128), 1)
    least = jnp.full((columns, 128), blocks << 16, jnp.int32)
    most = jnp.zeros((columns, 128), jnp.int32)
    for p in range(top):
        lists = metas[:, p, 0, :]
        key = (lanes + (p * per + 1)) * blocks + pltpu.roll(lists, 128 - per, 1)
        named = jnp.logical_and(lists == me, lanes < per)
        least = jnp.minimum(least, jnp.where(named, key, blocks << 16))
        most = jnp.maximum(most, jnp.where(named, key, 0))
    least = jnp.bitwise_and(jnp.min(least, axis=1, keepdims=True), blocks - 1)
    most = jnp.bitwise_and(jnp.max(most, axis=1, keepdims=True), blocks - 1)
    found[...] = jnp.where(lanes == 0, least, most)
    to_table = pltpu.make_async_copy(found, table, local_sem.at[2])
    to_table.start()
    to_table.wait()

    @pl.when(is_enc)
    def _():
        base_own.wait()

    @pl.when(is_dec)
    def _():
        base_copy(0).wait_recv()

    def fill(j, carry):
        for r in range(2):
            send[j, r] = share[table[j, r]]
        return carry

    lax.fori_loop(0, columns, fill, 0)
    for r in range(2):
        got[2 * me + r] = share[table[me, r]]

    def slot_copy(d):
        to = lax.rem(me + d, columns)
        return pltpu.make_async_remote_copy(
            src_ref=send.at[to],
            dst_ref=got.at[pl.ds(2 * me, 2)],
            send_sem=slot_send.at[d],
            recv_sem=slot_recv.at[columns - d],
            device_id={"dp": to},
            device_id_type=MESH,
        )

    each(lambda d: slot_copy(d).start())

    to_scalar.wait()
    names = [smeta[me, q // per, 0, q % per] for q in range(top * per)]
    for q in range(top * per):
        again = jnp.int32(0)
        for e in range(q):
            again = jnp.where(names[e] == names[q], 1, again)
        place[q] = 2 * names[q] + again
    mine = jnp.minimum(pool, top - 1)
    for k in range(per):
        lens[k] = smeta[smeta[me, mine, 0, k], top, 0, 2 * per + smeta[me, mine, 0, per + k]]

    ad_ref[...] = jnp.zeros_like(ad_ref)
    cg_ref[...] = jnp.zeros_like(cg_ref)

    @pl.when(is_enc)
    def _():
        out_ref[...] = jnp.zeros_like(out_ref)
        dq_ref[...] = jnp.zeros_like(dq_ref)
        for p in range(top):
            base_copy(p).wait_send()

    each(lambda d: slot_copy(d).wait_recv())

    def pick_copy(p, c):
        return pltpu.make_async_remote_copy(
            src_ref=pick.at[pl.ds(p * per + c * nbr, nbr)],
            dst_ref=blk.at[pool, pl.ds(c * nbr, nbr)],
            send_sem=pick_send.at[c, p],
            recv_sem=pick_recv.at[c, pool],
            device_id={"pool": p},
            device_id_type=MESH,
        )

    def pick_from(p, c):
        return pltpu.make_async_remote_copy(
            src_ref=pick.at[pl.ds(0, nbr)],
            dst_ref=blk.at[p, pl.ds(c * nbr, nbr)],
            send_sem=pick_send.at[c, p],
            recv_sem=pick_recv.at[c, p],
            device_id={"pool": p},
            device_id_type=MESH,
        )

    def choose(q, carry):
        pick[q] = got[place[q]]
        return carry

    lax.fori_loop(0, top * per, choose, 0)
    for k in range(per):
        blk[pool, k] = got[place[mine * per + k]]
    for c in range(spans):
        for p in range(top):

            @pl.when(pool != p)
            def _():
                pick_copy(p, c).start()

    def span(c, carry):
        for p in range(pools):

            @pl.when(pool != p)
            def _():
                pick_from(p, c).wait_recv()

        keys = nbr * slot_len
        scaling = HEAD ** (-0.5)
        at = pl.ds(pl.multiple_of(c * SPAN, SPAN), SPAN)
        rows = jnp.concatenate(
            [blk[p, c * nbr + n] for n in range(nbr) for p in range(pools)], axis=0
        ).astype(F32)
        cond = cond_ref[...].astype(F32)
        here = lax.broadcasted_iota(jnp.int32, cond.shape, 0) == c
        cond_row = jnp.sum(jnp.where(here, cond, 0.0), axis=0, keepdims=True)
        gain = gain_ref[...]
        x_full = rows + cond_row
        inv_rms = lax.rsqrt(jnp.mean(x_full * x_full, axis=-1, keepdims=True) + EPSILON)
        normed = x_full * inv_rms
        hidden = (normed * gain).astype(BF16)
        latent = dot_nn(hidden, wd_ref[...]).astype(BF16)
        encoded = (x_full + dot_nn(latent, wu_ref[...])).astype(BF16)
        for t in range(2 * hq // 512):
            cols = pl.ds(t * 512, 512)
            kv[:, cols] = dot_nn(encoded, wkv_ref[:, cols]).astype(BF16)

        slot = lax.broadcasted_iota(jnp.int32, (SPAN, keys), 1)
        bound = jnp.where(slot < slot_len, lens[c * nbr], lens[c * nbr + 1] + slot_len)
        usable = slot < bound

        def score(h):
            qs = pl.ds(h * HEAD, HEAD)
            vs = pl.ds(hq + h * HEAD, HEAD)
            s = dot_nt(q_ref[at, qs], kv[:, qs])
            dp = dot_nt(do_ref[at, qs], kv[:, vs])
            return s, dp

        def weigh(s, dp):
            s = jnp.where(usable, s * scaling, FLOOR)
            e = jnp.exp(s - jnp.max(s, axis=-1, keepdims=True))
            p = e * (1.0 / jnp.sum(e, axis=-1, keepdims=True))
            pdp = p * dp
            delta = jnp.sum(pdp, axis=-1, keepdims=True)
            return p.astype(BF16), (pdp - p * delta).astype(BF16)

        def finish(h, pb, ds):
            qs = pl.ds(h * HEAD, HEAD)
            vs = pl.ds(hq + h * HEAD, HEAD)
            out_ref[at, qs] = dot_nn(pb, kv[:, vs]).astype(BF16)
            dq_ref[at, qs] = (dot_nn(ds, kv[:, qs]) * scaling).astype(BF16)
            kvg[:, qs] = (dot_tn(ds, q_ref[at, qs]) * scaling).astype(BF16)
            kvg[:, vs] = dot_tn(pb, do_ref[at, qs]).astype(BF16)

        heads = hq // HEAD
        first, second = {}, {}
        for i in range(heads + 2 * STAGE):
            if i < heads:
                first[i] = score(i)
            if 0 <= i - STAGE < heads:
                second[i - STAGE] = weigh(*first.pop(i - STAGE))
            if 0 <= i - 2 * STAGE < heads:
                finish(i - 2 * STAGE, *second.pop(i - 2 * STAGE))

        enc_grad = dot_nt(kvg[...], wkv_ref[...]).astype(BF16)
        lat_grad = dot_nt(enc_grad, wu_ref[...]).astype(BF16)
        scaled = dot_nt(lat_grad, wd_ref[...]) * gain
        mean = jnp.mean(scaled * normed, axis=-1, keepdims=True)
        x_grad = enc_grad.astype(F32) + inv_rms * (scaled - normed * mean)
        cg_ref[pl.ds(c, 1), :] = jnp.sum(x_grad, axis=0, keepdims=True)
        ad_ref[:, :rank] += dot_tn(hidden, lat_grad)
        ad_ref[:, rank:] += dot_tn(enc_grad, latent)
        return carry

    def a_copy(d):
        to = lax.rem(me + d, columns)
        return pltpu.make_async_remote_copy(
            src_ref=part.at[to],
            dst_ref=lands.at[me],
            send_sem=a_send.at[d],
            recv_sem=a_recv.at[columns - d],
            device_id={"dp": to},
            device_id_type=MESH,
        )

    def b_copy(p):
        return pltpu.make_async_remote_copy(
            src_ref=held.at[p],
            dst_ref=tops.at[pool],
            send_sem=b_send.at[p],
            recv_sem=b_recv.at[pool],
            device_id={"pool": p},
            device_id_type=MESH,
        )

    def b_from(p):
        return pltpu.make_async_remote_copy(
            src_ref=held.at[p],
            dst_ref=tops.at[p],
            send_sem=b_send.at[p],
            recv_sem=b_recv.at[p],
            device_id={"pool": p},
            device_id_type=MESH,
        )

    @pl.when(is_dec)
    def _():
        for load in loads:
            load.wait()
        lax.fori_loop(0, spans, span, 0)
        piece = part.shape[2]
        for j in range(columns):
            for p in range(pools):
                part[j, p] = ad_ref[pl.ds((p * columns + j) * piece, piece), :].astype(BF16)
        each(lambda d: a_copy(d).start())
        lands[me] = part[me]

    each(lambda d: slot_copy(d).wait_send())
    for c in range(spans):
        for p in range(top):

            @pl.when(pool != p)
            def _():
                pick_copy(p, c).wait_send()

    @pl.when(is_dec)
    def _():
        each(lambda d: a_copy(d).wait())

        def add(j, total):
            return total + lands[j].astype(F32)

        held[...] = lax.fori_loop(1, columns, add, lands[0].astype(F32))
        for p in range(pools):

            @pl.when(pool != p)
            def _():
                b_copy(p).start()

            @pl.when(pool == p)
            def _():
                tops[p] = held[p]

        for p in range(pools):

            @pl.when(pool != p)
            def _():
                b_copy(p).wait_send()

    for p in range(top):

        @pl.when(pool != p)
        def _():
            b_from(p).wait_recv()

    total = tops[0]
    for p in range(1, top):
        total = total + tops[p]
    sum_ref[...] = total


def body(
    queries, cotangent, cond, nbr_owner, nbr_block, database, lengths, gain, w_down, w_up, w_kv
):
    pools = lax.axis_size("pool")
    columns = lax.axis_size("dp")
    tokens, hq = queries.shape[2:]
    spans, width = cond.shape[2:]
    nbr = nbr_owner.shape[3]
    blocks, slot_len = database.shape[2:4]
    rank = w_down.shape[1]
    per = spans * nbr
    quarter = slot_len // pools
    live = (pools - 1) * per
    piece = width // (pools * columns)
    dma = pltpu.SemaphoreType.DMA
    vmem = pl.BlockSpec(memory_space=pltpu.VMEM)
    smem = pl.BlockSpec(memory_space=pltpu.SMEM)
    where = pl.BlockSpec(memory_space=pl.ANY)
    attn_out, q_grad, cond_grad, adapter_grad = pl.pallas_call(
        functools.partial(whole_kernel, pools, columns),
        out_shape=(
            jax.ShapeDtypeStruct((tokens, hq), BF16),
            jax.ShapeDtypeStruct((tokens, hq), BF16),
            jax.ShapeDtypeStruct((spans, width), F32),
            jax.ShapeDtypeStruct((piece, 2 * rank), F32),
        ),
        in_specs=[smem, smem, smem, where, where, where, vmem, vmem, where, where, where],
        out_specs=(vmem, vmem, vmem, vmem),
        scratch_shapes=[
            pltpu.VMEM((1, 128), jnp.int32),
            pltpu.VMEM((columns, pools, 1, 128), jnp.int32),
            pltpu.SMEM((columns, pools, 1, 128), jnp.int32),
            pltpu.VMEM((columns, 128), jnp.int32),
            pltpu.SMEM((columns, 128), jnp.int32),
            pltpu.SMEM((live,), jnp.int32),
            pltpu.SMEM((per,), jnp.int32),
            pltpu.VMEM((blocks, quarter, width), BF16),
            pltpu.VMEM((columns, 2, quarter, width), BF16),
            pltpu.VMEM((2 * columns, quarter, width), BF16),
            pltpu.VMEM((live, quarter, width), BF16),
            pltpu.VMEM((pools, per, quarter, width), BF16),
            pltpu.VMEM((tokens, hq), BF16),
            pltpu.VMEM((tokens, hq), BF16),
            pltpu.VMEM((width, rank), BF16),
            pltpu.VMEM((rank, width), BF16),
            pltpu.VMEM((width, 2 * hq), BF16),
            pltpu.VMEM((nbr * slot_len, 2 * hq), BF16),
            pltpu.VMEM((nbr * slot_len, 2 * hq), BF16),
            pltpu.VMEM((width, 2 * rank), F32),
            pltpu.VMEM((columns, pools, piece, 2 * rank), BF16),
            pltpu.VMEM((columns, pools, piece, 2 * rank), BF16),
            pltpu.VMEM((pools, piece, 2 * rank), F32),
            pltpu.VMEM((pools, piece, 2 * rank), F32),
            dma((5,)),
            dma((3,)),
            dma((pools,)),
            dma,
            dma((pools,)),
            dma((pools,)),
            dma((columns,)),
            dma((columns,)),
            dma((columns,)),
            dma((columns,)),
            dma((spans, pools)),
            dma((spans, pools)),
            dma((columns,)),
            dma((columns,)),
            dma((pools,)),
            dma((pools,)),
        ],
        compiler_params=pltpu.CompilerParams(
            collective_id=0, has_side_effects=True, vmem_limit_bytes=60 << 20
        ),
        name="whole",
    )(
        nbr_owner.reshape(spans, nbr).T,
        nbr_block.reshape(spans, nbr).T,
        lengths.reshape(1, blocks),
        database.reshape(blocks, slot_len, width),
        queries.reshape(tokens, hq),
        cotangent.reshape(tokens, hq),
        cond.reshape(spans, width),
        gain.reshape(1, width),
        w_down,
        w_up,
        w_kv,
    )
    return (
        attn_out.reshape(1, 1, tokens, hq),
        q_grad.reshape(1, 1, tokens, hq),
        cond_grad.reshape(1, 1, spans, width),
        adapter_grad,
    )


def solution(mesh):
    return jax.shard_map(
        body,
        mesh=mesh,
        in_specs=(
            P("pool", "dp", None, None),
            P("pool", "dp", None, None),
            P("pool", "dp", None, None),
            P("pool", "dp", None, None),
            P("pool", "dp", None, None),
            P("pool", "dp", None, None, None),
            P("pool", "dp", None),
            P(),
            P(),
            P(),
            P(),
        ),
        out_specs=(
            P("pool", "dp", None, None),
            P("pool", "dp", None, None),
            P("pool", "dp", None, None),
            P(("pool", "dp"), None),
        ),
        check_vma=False,
    )
```

```python
import functools

import jax
import jax.numpy as jnp
from jax import lax
from jax.experimental import pallas as pl
from jax.experimental.pallas import tpu as pltpu
from jax.sharding import PartitionSpec as P

HEAD = 128
SPAN = 64
EPSILON = 1e-06
FLOOR = -1e30
STAGE = 4
F32 = jnp.float32
BF16 = jnp.bfloat16
MESH = pl.DeviceIdType.MESH


def dot_nn(a, b):
    return lax.dot_general(a, b, (((1,), (0,)), ((), ())), preferred_element_type=F32)


def dot_nt(a, b):
    return lax.dot_general(a, b, (((1,), (1,)), ((), ())), preferred_element_type=F32)


def dot_tn(a, b):
    return lax.dot_general(a, b, (((0,), (0,)), ((), ())), preferred_element_type=F32)


def greet(pools, columns):
    pool, me = lax.axis_index("pool"), lax.axis_index("dp")
    barrier = pltpu.get_barrier_semaphore()

    def hello(d, carry):
        pl.semaphore_signal(
            barrier, inc=1, device_id={"dp": lax.rem(me + d, columns)}, device_id_type=MESH
        )
        return carry

    lax.fori_loop(1, columns, hello, 0)
    for d in range(1, pools):
        pl.semaphore_signal(
            barrier, inc=1, device_id={"pool": lax.rem(pool + d, pools)}, device_id_type=MESH
        )
    pl.semaphore_wait(barrier, columns - 1 + pools - 1)


def whole_kernel(
    pools, columns,
    owner_ref, block_ref, len_ref, db_ref, q_hbm, do_hbm, cond_ref, gain_ref, wd_hbm, wu_hbm,
    wkv_hbm,
    out_hbm, dq_hbm, cg_ref, sum_ref,
    out_ref, dq_ref, row, metas, smeta, found, table, place, lens, share, send, got, pick, blk,
    q_ref, do_ref, wd_ref, wu_ref, wkv_ref, kv, kvg, ad_ref, part, lands, held, tops,
    load_sem, store_sem, local_sem, base_send, base_recv, row_send, row_recv, meta_send, meta_recv,
    slot_send, slot_recv, pick_send, pick_recv, a_send, a_recv, b_send, b_recv,
):
    pool, me = lax.axis_index("pool"), lax.axis_index("dp")
    top = pools - 1
    nbr, spans = owner_ref.shape
    per = spans * nbr
    blocks, quarter, width = share.shape
    hq = q_ref.shape[1]
    rank = wd_ref.shape[1]
    slot_len = pools * quarter
    is_enc = pool == top
    is_dec = jnp.logical_not(is_enc)

    loads = [
        pltpu.make_async_copy(a, b, load_sem.at[i])
        for i, (a, b) in enumerate(
            ((wd_hbm, wd_ref), (wu_hbm, wu_ref), (wkv_hbm, wkv_ref), (q_hbm, q_ref), (do_hbm, do_ref))
        )
    ]

    @pl.when(is_dec)
    def _():
        for load in loads:
            load.start()

    def each(action):
        def step(d, carry):
            action(d)
            return carry

        lax.fori_loop(1, columns, step, 0)

    lane = lax.broadcasted_iota(jnp.int32, (1, 128), 1)
    line = jnp.zeros((1, 128), jnp.int32)
    for k in range(per):
        line = jnp.where(lane == k, owner_ref[k % nbr, k // nbr], line)
        line = jnp.where(lane == per + k, block_ref[k % nbr, k // nbr], line)
    for k in range(blocks):
        line = jnp.where(lane == 2 * per + k, len_ref[0, k], line)
    row[...] = line
    metas[me, pool] = line
    greet(pools, columns)

    def row_copy(d):
        return pltpu.make_async_remote_copy(
            src_ref=row,
            dst_ref=metas.at[me, pool],
            send_sem=row_send.at[d],
            recv_sem=row_recv.at[pools - d],
            device_id={"pool": lax.rem(pool + d, pools)},
            device_id_type=MESH,
        )

    for d in range(1, pools):
        row_copy(d).start()

    early = blocks // 4
    halves = (pl.ds(0, early), pl.ds(early, blocks - early))

    def base_copy(p, half):
        return pltpu.make_async_remote_copy(
            src_ref=db_ref.at[halves[half], pl.ds(p * quarter, quarter), :],
            dst_ref=share.at[halves[half]],
            send_sem=base_send.at[half, p],
            recv_sem=base_recv.at[half],
            device_id={"pool": p},
            device_id_type=MESH,
        )

    base_own = pltpu.make_async_copy(
        db_ref.at[:, pl.ds(top * quarter, quarter), :], share, local_sem.at[0]
    )

    @pl.when(is_enc)
    def _():
        for p in range(top):
            base_copy(p, 0).start()
        base_own.start()

    for d in range(1, pools):
        row_copy(d).wait()

    def meta_copy(d):
        return pltpu.make_async_remote_copy(
            src_ref=metas.at[me],
            dst_ref=metas.at[me],
            send_sem=meta_send.at[d],
            recv_sem=meta_recv.at[columns - d],
            device_id={"dp": lax.rem(me + d, columns)},
            device_id_type=MESH,
        )

    each(lambda d: meta_copy(d).start())

    @pl.when(is_enc)
    def _():
        for p in range(top):
            base_copy(p, 1).start()


    each(lambda d: meta_copy(d).wait())
    to_scalar = pltpu.make_async_copy(metas, smeta, local_sem.at[1])
    to_scalar.start()

    lanes = lax.broadcasted_iota(jnp.int32, (columns, 128), 1)
    least = jnp.full((columns, 128), blocks << 16, jnp.int32)
    most = jnp.zeros((columns, 128), jnp.int32)
    for p in range(top):
        lists = metas[:, p, 0, :]
        key = (lanes + (p * per + 1)) * blocks + pltpu.roll(lists, 128 - per, 1)
        named = jnp.logical_and(lists == me, lanes < per)
        least = jnp.minimum(least, jnp.where(named, key, blocks << 16))
        most = jnp.maximum(most, jnp.where(named, key, 0))
    least = jnp.bitwise_and(jnp.min(least, axis=1, keepdims=True), blocks - 1)
    most = jnp.bitwise_and(jnp.max(most, axis=1, keepdims=True), blocks - 1)
    found[...] = jnp.where(lanes == 0, least, most)
    to_table = pltpu.make_async_copy(found, table, local_sem.at[2])
    to_table.start()
    to_table.wait()

    @pl.when(is_enc)
    def _():
        base_own.wait()

    @pl.when(is_dec)
    def _():
        base_copy(0, 0).wait_recv()
        base_copy(0, 1).wait_recv()

    def fill(j, carry):
        for r in range(2):
            send[j, r] = share[table[j, r]]
        return carry

    lax.fori_loop(0, columns, fill, 0)
    for r in range(2):
        got[2 * me + r] = share[table[me, r]]

    def slot_copy(d):
        to = lax.rem(me + d, columns)
        return pltpu.make_async_remote_copy(
            src_ref=send.at[to],
            dst_ref=got.at[pl.ds(2 * me, 2)],
            send_sem=slot_send.at[d],
            recv_sem=slot_recv.at[columns - d],
            device_id={"dp": to},
            device_id_type=MESH,
        )

    each(lambda d: slot_copy(d).start())

    to_scalar.wait()
    names = [smeta[me, q // per, 0, q % per] for q in range(top * per)]
    for q in range(top * per):
        again = jnp.int32(0)
        for e in range(q):
            again = jnp.where(names[e] == names[q], 1, again)
        place[q] = 2 * names[q] + again
    mine = jnp.minimum(pool, top - 1)
    for k in range(per):
        lens[k] = smeta[smeta[me, mine, 0, k], top, 0, 2 * per + smeta[me, mine, 0, per + k]]

    ad_ref[...] = jnp.zeros_like(ad_ref)
    cg_ref[...] = jnp.zeros_like(cg_ref)

    def stores(c):
        at = pl.ds(pl.multiple_of(c * SPAN, SPAN), SPAN)
        return (
            pltpu.make_async_copy(out_ref.at[at], out_hbm.at[at], store_sem.at[c, 0]),
            pltpu.make_async_copy(dq_ref.at[at], dq_hbm.at[at], store_sem.at[c, 1]),
        )

    @pl.when(is_enc)
    def _():
        out_ref[...] = jnp.zeros_like(out_ref)
        dq_ref[...] = jnp.zeros_like(dq_ref)
        for p in range(top):
            for part_of in range(2):
                base_copy(p, part_of).wait_send()
        for c in range(spans):
            for store in stores(c):
                store.start()

    each(lambda d: slot_copy(d).wait_recv())

    def pick_copy(p, c):
        return pltpu.make_async_remote_copy(
            src_ref=pick.at[pl.ds(p * per + c * nbr, nbr)],
            dst_ref=blk.at[pool, pl.ds(c * nbr, nbr)],
            send_sem=pick_send.at[c, p],
            recv_sem=pick_recv.at[c, pool],
            device_id={"pool": p},
            device_id_type=MESH,
        )

    def pick_from(p, c):
        return pltpu.make_async_remote_copy(
            src_ref=pick.at[pl.ds(0, nbr)],
            dst_ref=blk.at[p, pl.ds(c * nbr, nbr)],
            send_sem=pick_send.at[c, p],
            recv_sem=pick_recv.at[c, p],
            device_id={"pool": p},
            device_id_type=MESH,
        )

    def choose(q, carry):
        pick[q] = got[place[q]]
        return carry

    lax.fori_loop(0, top * per, choose, 0)
    for k in range(per):
        blk[pool, k] = got[place[mine * per + k]]
    for c in range(spans):
        for p in range(top):

            @pl.when(pool != p)
            def _():
                pick_copy(p, c).start()

    def span(c, carry):
        for p in range(pools):

            @pl.when(pool != p)
            def _():
                pick_from(p, c).wait_recv()

        @pl.when(c > 0)
        def _():
            for store in stores(c - 1):
                store.start()

        keys = nbr * slot_len
        scaling = HEAD ** (-0.5)
        at = pl.ds(pl.multiple_of(c * SPAN, SPAN), SPAN)
        rows = jnp.concatenate(
            [blk[p, c * nbr + n] for n in range(nbr) for p in range(pools)], axis=0
        ).astype(F32)
        cond = cond_ref[...].astype(F32)
        here = lax.broadcasted_iota(jnp.int32, cond.shape, 0) == c
        cond_row = jnp.sum(jnp.where(here, cond, 0.0), axis=0, keepdims=True)
        gain = gain_ref[...]
        x_full = rows + cond_row
        inv_rms = lax.rsqrt(jnp.mean(x_full * x_full, axis=-1, keepdims=True) + EPSILON)
        normed = x_full * inv_rms
        hidden = (normed * gain).astype(BF16)
        latent = dot_nn(hidden, wd_ref[...]).astype(BF16)
        encoded = (x_full + dot_nn(latent, wu_ref[...])).astype(BF16)
        for t in range(2 * hq // 512):
            cols = pl.ds(t * 512, 512)
            kv[:, cols] = dot_nn(encoded, wkv_ref[:, cols]).astype(BF16)

        slot = lax.broadcasted_iota(jnp.int32, (SPAN, keys), 1)
        bound = jnp.where(slot < slot_len, lens[c * nbr], lens[c * nbr + 1] + slot_len)
        usable = slot < bound

        def score(h):
            qs = pl.ds(h * HEAD, HEAD)
            vs = pl.ds(hq + h * HEAD, HEAD)
            s = dot_nt(q_ref[at, qs], kv[:, qs])
            dp = dot_nt(do_ref[at, qs], kv[:, vs])
            return s, dp

        def weigh(s, dp):
            s = jnp.where(usable, s * scaling, FLOOR)
            e = jnp.exp(s - jnp.max(s, axis=-1, keepdims=True))
            p = e * (1.0 / jnp.sum(e, axis=-1, keepdims=True))
            pdp = p * dp
            delta = jnp.sum(pdp, axis=-1, keepdims=True)
            return p.astype(BF16), (pdp - p * delta).astype(BF16)

        def finish(h, pb, ds):
            qs = pl.ds(h * HEAD, HEAD)
            vs = pl.ds(hq + h * HEAD, HEAD)
            out_ref[at, qs] = dot_nn(pb, kv[:, vs]).astype(BF16)
            dq_ref[at, qs] = (dot_nn(ds, kv[:, qs]) * scaling).astype(BF16)
            kvg[:, qs] = (dot_tn(ds, q_ref[at, qs]) * scaling).astype(BF16)
            kvg[:, vs] = dot_tn(pb, do_ref[at, qs]).astype(BF16)

        heads = hq // HEAD
        first, second = {}, {}
        for i in range(heads + 2 * STAGE):
            if i < heads:
                first[i] = score(i)
            if 0 <= i - STAGE < heads:
                second[i - STAGE] = weigh(*first.pop(i - STAGE))
            if 0 <= i - 2 * STAGE < heads:
                finish(i - 2 * STAGE, *second.pop(i - 2 * STAGE))

        enc_grad = dot_nt(kvg[...], wkv_ref[...]).astype(BF16)
        lat_grad = dot_nt(enc_grad, wu_ref[...]).astype(BF16)
        scaled = dot_nt(lat_grad, wd_ref[...]) * gain
        mean = jnp.mean(scaled * normed, axis=-1, keepdims=True)
        x_grad = enc_grad.astype(F32) + inv_rms * (scaled - normed * mean)
        cg_ref[pl.ds(c, 1), :] = jnp.sum(x_grad, axis=0, keepdims=True)
        ad_ref[:, :rank] += dot_tn(hidden, lat_grad)
        ad_ref[:, rank:] += dot_tn(enc_grad, latent)
        return carry

    def a_copy(d):
        to = lax.rem(me + d, columns)
        return pltpu.make_async_remote_copy(
            src_ref=part.at[to],
            dst_ref=lands.at[me],
            send_sem=a_send.at[d],
            recv_sem=a_recv.at[columns - d],
            device_id={"dp": to},
            device_id_type=MESH,
        )

    def b_copy(p):
        return pltpu.make_async_remote_copy(
            src_ref=held.at[p],
            dst_ref=tops.at[pool],
            send_sem=b_send.at[p],
            recv_sem=b_recv.at[pool],
            device_id={"pool": p},
            device_id_type=MESH,
        )

    def b_from(p):
        return pltpu.make_async_remote_copy(
            src_ref=held.at[p],
            dst_ref=tops.at[p],
            send_sem=b_send.at[p],
            recv_sem=b_recv.at[p],
            device_id={"pool": p},
            device_id_type=MESH,
        )

    @pl.when(is_dec)
    def _():
        for load in loads:
            load.wait()
        lax.fori_loop(0, spans, span, 0)
        for store in stores(spans - 1):
            store.start()
        piece = part.shape[2]
        for j in range(columns):
            for p in range(pools):
                part[j, p] = ad_ref[pl.ds((p * columns + j) * piece, piece), :].astype(BF16)
        each(lambda d: a_copy(d).start())
        lands[me] = part[me]

    for c in range(spans):
        for store in stores(c):
            store.wait()

    each(lambda d: slot_copy(d).wait_send())
    for c in range(spans):
        for p in range(top):

            @pl.when(pool != p)
            def _():
                pick_copy(p, c).wait_send()

    @pl.when(is_dec)
    def _():
        each(lambda d: a_copy(d).wait())

        def add(j, total):
            return total + lands[j].astype(F32)

        held[...] = lax.fori_loop(1, columns, add, lands[0].astype(F32))
        for p in range(pools):

            @pl.when(pool != p)
            def _():
                b_copy(p).start()

            @pl.when(pool == p)
            def _():
                tops[p] = held[p]

        for p in range(pools):

            @pl.when(pool != p)
            def _():
                b_copy(p).wait_send()

    for p in range(top):

        @pl.when(pool != p)
        def _():
            b_from(p).wait_recv()

    total = tops[0]
    for p in range(1, top):
        total = total + tops[p]
    sum_ref[...] = total


def flush_kernel(chunks, *refs):
    n = len(chunks)
    sources, targets, bounces = refs[:n], refs[n : 2 * n], refs[2 * n : 3 * n]
    in_sem, out_sem = refs[3 * n :]
    steps = []
    for i in range(n):
        size = sources[i].shape[0] // chunks[i]
        for t in range(chunks[i]):
            at = pl.ds(t * size, size)
            k = len(steps)
            steps.append(
                (
                    pltpu.make_async_copy(sources[i].at[at], bounces[i].at[at], in_sem.at[k]),
                    pltpu.make_async_copy(bounces[i].at[at], targets[i].at[at], out_sem.at[k]),
                )
            )
    for load, _ in steps:
        load.start()
    for load, store in steps:
        load.wait()
        store.start()
    for _, store in steps:
        store.wait()


def flush(chunks, *arrays):
    where = pl.BlockSpec(memory_space=pl.ANY)
    return pl.pallas_call(
        functools.partial(flush_kernel, chunks),
        out_shape=tuple(jax.ShapeDtypeStruct(a.shape, a.dtype) for a in arrays),
        in_specs=[where] * len(arrays),
        out_specs=(where,) * len(arrays),
        scratch_shapes=[pltpu.VMEM(a.shape, a.dtype) for a in arrays]
        + [pltpu.SemaphoreType.DMA((sum(chunks),))] * 2,
        compiler_params=pltpu.CompilerParams(vmem_limit_bytes=60 << 20),
        name="flush",
    )(*arrays)


def body(
    queries, cotangent, cond, nbr_owner, nbr_block, database, lengths, gain, w_down, w_up, w_kv
):
    pools = lax.axis_size("pool")
    columns = lax.axis_size("dp")
    tokens, hq = queries.shape[2:]
    spans, width = cond.shape[2:]
    nbr = nbr_owner.shape[3]
    blocks, slot_len = database.shape[2:4]
    rank = w_down.shape[1]
    per = spans * nbr
    quarter = slot_len // pools
    live = (pools - 1) * per
    piece = width // (pools * columns)
    dma = pltpu.SemaphoreType.DMA
    vmem = pl.BlockSpec(memory_space=pltpu.VMEM)
    smem = pl.BlockSpec(memory_space=pltpu.SMEM)
    where = pl.BlockSpec(memory_space=pl.ANY)
    attn_out, q_grad, cond_grad, adapter_grad = pl.pallas_call(
        functools.partial(whole_kernel, pools, columns),
        out_shape=(
            jax.ShapeDtypeStruct((tokens, hq), BF16),
            jax.ShapeDtypeStruct((tokens, hq), BF16),
            jax.ShapeDtypeStruct((spans, width), F32),
            jax.ShapeDtypeStruct((piece, 2 * rank), F32),
        ),
        in_specs=[smem, smem, smem, where, where, where, vmem, vmem, where, where, where],
        out_specs=(where, where, vmem, vmem),
        scratch_shapes=[
            pltpu.VMEM((tokens, hq), BF16),
            pltpu.VMEM((tokens, hq), BF16),
            pltpu.VMEM((1, 128), jnp.int32),
            pltpu.VMEM((columns, pools, 1, 128), jnp.int32),
            pltpu.SMEM((columns, pools, 1, 128), jnp.int32),
            pltpu.VMEM((columns, 128), jnp.int32),
            pltpu.SMEM((columns, 128), jnp.int32),
            pltpu.SMEM((live,), jnp.int32),
            pltpu.SMEM((per,), jnp.int32),
            pltpu.VMEM((blocks, quarter, width), BF16),
            pltpu.VMEM((columns, 2, quarter, width), BF16),
            pltpu.VMEM((2 * columns, quarter, width), BF16),
            pltpu.VMEM((live, quarter, width), BF16),
            pltpu.VMEM((pools, per, quarter, width), BF16),
            pltpu.VMEM((tokens, hq), BF16),
            pltpu.VMEM((tokens, hq), BF16),
            pltpu.VMEM((width, rank), BF16),
            pltpu.VMEM((rank, width), BF16),
            pltpu.VMEM((width, 2 * hq), BF16),
            pltpu.VMEM((nbr * slot_len, 2 * hq), BF16),
            pltpu.VMEM((nbr * slot_len, 2 * hq), BF16),
            pltpu.VMEM((width, 2 * rank), F32),
            pltpu.VMEM((columns, pools, piece, 2 * rank), BF16),
            pltpu.VMEM((columns, pools, piece, 2 * rank), BF16),
            pltpu.VMEM((pools, piece, 2 * rank), F32),
            pltpu.VMEM((pools, piece, 2 * rank), F32),
            dma((5,)),
            dma((spans, 2)),
            dma((3,)),
            dma((2, pools)),
            dma((2,)),
            dma((pools,)),
            dma((pools,)),
            dma((columns,)),
            dma((columns,)),
            dma((columns,)),
            dma((columns,)),
            dma((spans, pools)),
            dma((spans, pools)),
            dma((columns,)),
            dma((columns,)),
            dma((pools,)),
            dma((pools,)),
        ],
        compiler_params=pltpu.CompilerParams(
            collective_id=0, has_side_effects=True, vmem_limit_bytes=60 << 20
        ),
        name="whole",
    )(
        nbr_owner.reshape(spans, nbr).T,
        nbr_block.reshape(spans, nbr).T,
        lengths.reshape(1, blocks),
        database.reshape(blocks, slot_len, width),
        queries.reshape(tokens, hq),
        cotangent.reshape(tokens, hq),
        cond.reshape(spans, width),
        gain.reshape(1, width),
        w_down,
        w_up,
        w_kv,
    )
    attn_out, q_grad, cond_grad, adapter_grad = flush(
        (4, 4, 1, 1), attn_out, q_grad, cond_grad, adapter_grad
    )
    return (
        attn_out.reshape(1, 1, tokens, hq),
        q_grad.reshape(1, 1, tokens, hq),
        cond_grad.reshape(1, 1, spans, width),
        adapter_grad,
    )


def solution(mesh):
    return jax.shard_map(
        body,
        mesh=mesh,
        in_specs=(
            P("pool", "dp", None, None),
            P("pool", "dp", None, None),
            P("pool", "dp", None, None),
            P("pool", "dp", None, None),
            P("pool", "dp", None, None),
            P("pool", "dp", None, None, None),
            P("pool", "dp", None),
            P(),
            P(),
            P(),
            P(),
        ),
        out_specs=(
            P("pool", "dp", None, None),
            P("pool", "dp", None, None),
            P("pool", "dp", None, None),
            P(("pool", "dp"), None),
        ),
        check_vma=False,
    )
```

```python
import functools

import jax
import jax.numpy as jnp
from jax import lax
from jax.experimental import pallas as pl
from jax.experimental.pallas import tpu as pltpu
from jax.sharding import PartitionSpec as P

HEAD = 128
SPAN = 64
EPSILON = 1e-06
FLOOR = -1e30
STAGE = 4
GRID = (4, 2, 4)
ORDER = ((3, 1, 1), (2, 0, 2), (1, 1, 0), (1, 0, 3), (3, 0, 3), (0, 0, 2), (0, 1, 2), (3, 1, 3), (1, 0, 0), (2, 0, 1), (1, 0, 2), (2, 1, 0), (3, 1, 2), (1, 1, 2), (2, 1, 2), (0, 0, 1), (2, 1, 1), (3, 0, 0), (0, 1, 3), (1, 1, 1), (2, 1, 3), (1, 1, 3), (2, 0, 0), (0, 1, 0), (1, 0, 1), (0, 0, 3), (3, 0, 1), (3, 0, 2), (3, 1, 0), (2, 0, 3), (0, 1, 1))
F32 = jnp.float32
BF16 = jnp.bfloat16
MESH = pl.DeviceIdType.MESH


def dot_nn(a, b):
    return lax.dot_general(a, b, (((1,), (0,)), ((), ())), preferred_element_type=F32)


def dot_nt(a, b):
    return lax.dot_general(a, b, (((1,), (1,)), ((), ())), preferred_element_type=F32)


def dot_tn(a, b):
    return lax.dot_general(a, b, (((0,), (0,)), ((), ())), preferred_element_type=F32)


def shifted(me, step):
    z, x, y = me // (GRID[1] * GRID[2]), lax.rem(me // GRID[2], GRID[1]), lax.rem(me, GRID[2])
    z, x, y = (lax.rem(c + d, n) for c, d, n in zip((z, x, y), step, GRID))
    return (z * GRID[1] + x) * GRID[2] + y


def greet(pools, columns):
    pool, me = lax.axis_index("pool"), lax.axis_index("dp")
    barrier = pltpu.get_barrier_semaphore()

    def hello(d, carry):
        pl.semaphore_signal(
            barrier, inc=1, device_id={"dp": lax.rem(me + d, columns)}, device_id_type=MESH
        )
        return carry

    lax.fori_loop(1, columns, hello, 0)
    for d in range(1, pools):
        pl.semaphore_signal(
            barrier, inc=1, device_id={"pool": lax.rem(pool + d, pools)}, device_id_type=MESH
        )
    pl.semaphore_wait(barrier, columns - 1 + pools - 1)


def whole_kernel(
    pools, columns,
    owner_ref, block_ref, len_ref, db_ref, q_hbm, do_hbm, cond_ref, gain_ref, wd_hbm, wu_hbm,
    wkv_hbm,
    out_hbm, dq_hbm, cg_ref, sum_ref,
    out_ref, dq_ref, row, metas, smeta, found, table, place, lens, share, send, got, pick, blk,
    q_ref, do_ref, wd_ref, wu_ref, wkv_ref, kv, kvg, ad_ref, part, lands, held, tops,
    load_sem, store_sem, local_sem, base_send, base_recv, row_send, row_recv, meta_send, meta_recv,
    slot_send, slot_recv, pick_send, pick_recv, a_send, a_recv, b_send, b_recv,
):
    pool, me = lax.axis_index("pool"), lax.axis_index("dp")
    top = pools - 1
    nbr, spans = owner_ref.shape
    per = spans * nbr
    blocks, quarter, width = share.shape
    hq = q_ref.shape[1]
    rank = wd_ref.shape[1]
    slot_len = pools * quarter
    is_enc = pool == top
    is_dec = jnp.logical_not(is_enc)

    loads = [
        pltpu.make_async_copy(a, b, load_sem.at[i])
        for i, (a, b) in enumerate(
            ((wd_hbm, wd_ref), (wu_hbm, wu_ref), (wkv_hbm, wkv_ref), (q_hbm, q_ref), (do_hbm, do_ref))
        )
    ]

    @pl.when(is_dec)
    def _():
        for load in loads:
            load.start()

    def each(action):
        def step(d, carry):
            action(d)
            return carry

        lax.fori_loop(1, columns, step, 0)

    lane = lax.broadcasted_iota(jnp.int32, (1, 128), 1)
    line = jnp.zeros((1, 128), jnp.int32)
    for k in range(per):
        line = jnp.where(lane == k, owner_ref[k % nbr, k // nbr], line)
        line = jnp.where(lane == per + k, block_ref[k % nbr, k // nbr], line)
    for k in range(blocks):
        line = jnp.where(lane == 2 * per + k, len_ref[0, k], line)
    row[...] = line
    metas[me, pool] = line
    greet(pools, columns)

    def row_copy(d):
        return pltpu.make_async_remote_copy(
            src_ref=row,
            dst_ref=metas.at[me, pool],
            send_sem=row_send.at[d],
            recv_sem=row_recv.at[pools - d],
            device_id={"pool": lax.rem(pool + d, pools)},
            device_id_type=MESH,
        )

    for d in range(1, pools):
        row_copy(d).start()

    early = blocks // 4
    halves = (pl.ds(0, early), pl.ds(early, blocks - early))

    def base_copy(p, half):
        return pltpu.make_async_remote_copy(
            src_ref=db_ref.at[halves[half], pl.ds(p * quarter, quarter), :],
            dst_ref=share.at[halves[half]],
            send_sem=base_send.at[half, p],
            recv_sem=base_recv.at[half],
            device_id={"pool": p},
            device_id_type=MESH,
        )

    base_own = pltpu.make_async_copy(
        db_ref.at[:, pl.ds(top * quarter, quarter), :], share, local_sem.at[0]
    )

    @pl.when(is_enc)
    def _():
        for p in range(top):
            base_copy(p, 0).start()
        base_own.start()

    for d in range(1, pools):
        row_copy(d).wait()

    def meta_copy(d):
        return pltpu.make_async_remote_copy(
            src_ref=metas.at[me],
            dst_ref=metas.at[me],
            send_sem=meta_send.at[d],
            recv_sem=meta_recv.at[columns - d],
            device_id={"dp": lax.rem(me + d, columns)},
            device_id_type=MESH,
        )

    each(lambda d: meta_copy(d).start())

    @pl.when(is_enc)
    def _():
        for p in range(top):
            base_copy(p, 1).start()


    each(lambda d: meta_copy(d).wait())
    to_scalar = pltpu.make_async_copy(metas, smeta, local_sem.at[1])
    to_scalar.start()

    lanes = lax.broadcasted_iota(jnp.int32, (columns, 128), 1)
    least = jnp.full((columns, 128), blocks << 16, jnp.int32)
    most = jnp.zeros((columns, 128), jnp.int32)
    for p in range(top):
        lists = metas[:, p, 0, :]
        key = (lanes + (p * per + 1)) * blocks + pltpu.roll(lists, 128 - per, 1)
        named = jnp.logical_and(lists == me, lanes < per)
        least = jnp.minimum(least, jnp.where(named, key, blocks << 16))
        most = jnp.maximum(most, jnp.where(named, key, 0))
    least = jnp.bitwise_and(jnp.min(least, axis=1, keepdims=True), blocks - 1)
    most = jnp.bitwise_and(jnp.max(most, axis=1, keepdims=True), blocks - 1)
    found[...] = jnp.where(lanes == 0, least, most)
    to_table = pltpu.make_async_copy(found, table, local_sem.at[2])
    to_table.start()
    to_table.wait()

    @pl.when(is_enc)
    def _():
        base_own.wait()

    @pl.when(is_dec)
    def _():
        base_copy(0, 0).wait_recv()
        base_copy(0, 1).wait_recv()

    def fill(j, carry):
        for r in range(2):
            send[j, r] = share[table[j, r]]
        return carry

    lax.fori_loop(0, columns, fill, 0)
    for r in range(2):
        got[2 * me + r] = share[table[me, r]]

    def slot_copy(d):
        to = shifted(me, ORDER[d])
        return pltpu.make_async_remote_copy(
            src_ref=send.at[to],
            dst_ref=got.at[pl.ds(2 * me, 2)],
            send_sem=slot_send.at[d],
            recv_sem=slot_recv.at[d],
            device_id={"dp": to},
            device_id_type=MESH,
        )

    for d in range(columns - 1):
        slot_copy(d).start()

    to_scalar.wait()
    names = [smeta[me, q // per, 0, q % per] for q in range(top * per)]
    for q in range(top * per):
        again = jnp.int32(0)
        for e in range(q):
            again = jnp.where(names[e] == names[q], 1, again)
        place[q] = 2 * names[q] + again
    mine = jnp.minimum(pool, top - 1)
    for k in range(per):
        lens[k] = smeta[smeta[me, mine, 0, k], top, 0, 2 * per + smeta[me, mine, 0, per + k]]

    ad_ref[...] = jnp.zeros_like(ad_ref)
    cg_ref[...] = jnp.zeros_like(cg_ref)

    def stores(c):
        at = pl.ds(pl.multiple_of(c * SPAN, SPAN), SPAN)
        return (
            pltpu.make_async_copy(out_ref.at[at], out_hbm.at[at], store_sem.at[c, 0]),
            pltpu.make_async_copy(dq_ref.at[at], dq_hbm.at[at], store_sem.at[c, 1]),
        )

    @pl.when(is_enc)
    def _():
        out_ref[...] = jnp.zeros_like(out_ref)
        dq_ref[...] = jnp.zeros_like(dq_ref)
        for p in range(top):
            for part_of in range(2):
                base_copy(p, part_of).wait_send()
        for c in range(spans):
            for store in stores(c):
                store.start()

    for d in range(columns - 1):
        slot_copy(d).wait_recv()

    def pick_copy(p, c):
        return pltpu.make_async_remote_copy(
            src_ref=pick.at[pl.ds(p * per + c * nbr, nbr)],
            dst_ref=blk.at[pool, pl.ds(c * nbr, nbr)],
            send_sem=pick_send.at[c, p],
            recv_sem=pick_recv.at[c, pool],
            device_id={"pool": p},
            device_id_type=MESH,
        )

    def pick_from(p, c):
        return pltpu.make_async_remote_copy(
            src_ref=pick.at[pl.ds(0, nbr)],
            dst_ref=blk.at[p, pl.ds(c * nbr, nbr)],
            send_sem=pick_send.at[c, p],
            recv_sem=pick_recv.at[c, p],
            device_id={"pool": p},
            device_id_type=MESH,
        )

    def choose(q, carry):
        pick[q] = got[place[q]]
        return carry

    lax.fori_loop(0, top * per, choose, 0)
    for k in range(per):
        blk[pool, k] = got[place[mine * per + k]]
    for c in range(spans):
        for p in range(top):

            @pl.when(pool != p)
            def _():
                pick_copy(p, c).start()

    def span(c, carry):
        for p in range(pools):

            @pl.when(pool != p)
            def _():
                pick_from(p, c).wait_recv()

        @pl.when(c > 0)
        def _():
            for store in stores(c - 1):
                store.start()

        keys = nbr * slot_len
        scaling = HEAD ** (-0.5)
        at = pl.ds(pl.multiple_of(c * SPAN, SPAN), SPAN)
        rows = jnp.concatenate(
            [blk[p, c * nbr + n] for n in range(nbr) for p in range(pools)], axis=0
        ).astype(F32)
        cond = cond_ref[...].astype(F32)
        here = lax.broadcasted_iota(jnp.int32, cond.shape, 0) == c
        cond_row = jnp.sum(jnp.where(here, cond, 0.0), axis=0, keepdims=True)
        gain = gain_ref[...]
        x_full = rows + cond_row
        inv_rms = lax.rsqrt(jnp.mean(x_full * x_full, axis=-1, keepdims=True) + EPSILON)
        normed = x_full * inv_rms
        hidden = (normed * gain).astype(BF16)
        latent = dot_nn(hidden, wd_ref[...]).astype(BF16)
        encoded = (x_full + dot_nn(latent, wu_ref[...])).astype(BF16)
        for t in range(2 * hq // 512):
            cols = pl.ds(t * 512, 512)
            kv[:, cols] = dot_nn(encoded, wkv_ref[:, cols]).astype(BF16)

        slot = lax.broadcasted_iota(jnp.int32, (SPAN, keys), 1)
        bound = jnp.where(slot < slot_len, lens[c * nbr], lens[c * nbr + 1] + slot_len)
        usable = slot < bound

        def score(h):
            qs = pl.ds(h * HEAD, HEAD)
            vs = pl.ds(hq + h * HEAD, HEAD)
            s = dot_nt(q_ref[at, qs], kv[:, qs])
            dp = dot_nt(do_ref[at, qs], kv[:, vs])
            return s, dp

        def weigh(s, dp):
            s = jnp.where(usable, s * scaling, FLOOR)
            e = jnp.exp(s - jnp.max(s, axis=-1, keepdims=True))
            p = e * (1.0 / jnp.sum(e, axis=-1, keepdims=True))
            pdp = p * dp
            delta = jnp.sum(pdp, axis=-1, keepdims=True)
            return p.astype(BF16), (pdp - p * delta).astype(BF16)

        def finish(h, pb, ds):
            qs = pl.ds(h * HEAD, HEAD)
            vs = pl.ds(hq + h * HEAD, HEAD)
            out_ref[at, qs] = dot_nn(pb, kv[:, vs]).astype(BF16)
            dq_ref[at, qs] = (dot_nn(ds, kv[:, qs]) * scaling).astype(BF16)
            kvg[:, qs] = (dot_tn(ds, q_ref[at, qs]) * scaling).astype(BF16)
            kvg[:, vs] = dot_tn(pb, do_ref[at, qs]).astype(BF16)

        heads = hq // HEAD
        first, second = {}, {}
        for i in range(heads + 2 * STAGE):
            if i < heads:
                first[i] = score(i)
            if 0 <= i - STAGE < heads:
                second[i - STAGE] = weigh(*first.pop(i - STAGE))
            if 0 <= i - 2 * STAGE < heads:
                finish(i - 2 * STAGE, *second.pop(i - 2 * STAGE))

        enc_grad = dot_nt(kvg[...], wkv_ref[...]).astype(BF16)
        lat_grad = dot_nt(enc_grad, wu_ref[...]).astype(BF16)
        scaled = dot_nt(lat_grad, wd_ref[...]) * gain
        mean = jnp.mean(scaled * normed, axis=-1, keepdims=True)
        x_grad = enc_grad.astype(F32) + inv_rms * (scaled - normed * mean)
        cg_ref[pl.ds(c, 1), :] = jnp.sum(x_grad, axis=0, keepdims=True)
        ad_ref[:, :rank] += dot_tn(hidden, lat_grad)
        ad_ref[:, rank:] += dot_tn(enc_grad, latent)
        return carry

    def a_copy(d):
        to = shifted(me, ORDER[d])
        return pltpu.make_async_remote_copy(
            src_ref=part.at[to],
            dst_ref=lands.at[me],
            send_sem=a_send.at[d],
            recv_sem=a_recv.at[d],
            device_id={"dp": to},
            device_id_type=MESH,
        )

    def b_copy(p):
        return pltpu.make_async_remote_copy(
            src_ref=held.at[p],
            dst_ref=tops.at[pool],
            send_sem=b_send.at[p],
            recv_sem=b_recv.at[pool],
            device_id={"pool": p},
            device_id_type=MESH,
        )

    def b_from(p):
        return pltpu.make_async_remote_copy(
            src_ref=held.at[p],
            dst_ref=tops.at[p],
            send_sem=b_send.at[p],
            recv_sem=b_recv.at[p],
            device_id={"pool": p},
            device_id_type=MESH,
        )

    @pl.when(is_dec)
    def _():
        for load in loads:
            load.wait()
        lax.fori_loop(0, spans, span, 0)
        for store in stores(spans - 1):
            store.start()
        piece = part.shape[2]
        for j in range(columns):
            for p in range(pools):
                part[j, p] = ad_ref[pl.ds((p * columns + j) * piece, piece), :].astype(BF16)
        for d in range(columns - 1):
            a_copy(d).start()
        lands[me] = part[me]

    for c in range(spans):
        for store in stores(c):
            store.wait()

    for d in range(columns - 1):
        slot_copy(d).wait_send()
    for c in range(spans):
        for p in range(top):

            @pl.when(pool != p)
            def _():
                pick_copy(p, c).wait_send()

    @pl.when(is_dec)
    def _():
        for d in range(columns - 1):
            a_copy(d).wait()

        def add(j, total):
            return total + lands[j].astype(F32)

        held[...] = lax.fori_loop(1, columns, add, lands[0].astype(F32))
        for p in range(pools):

            @pl.when(pool != p)
            def _():
                b_copy(p).start()

            @pl.when(pool == p)
            def _():
                tops[p] = held[p]

        for p in range(pools):

            @pl.when(pool != p)
            def _():
                b_copy(p).wait_send()

    for p in range(top):

        @pl.when(pool != p)
        def _():
            b_from(p).wait_recv()

    total = tops[0]
    for p in range(1, top):
        total = total + tops[p]
    sum_ref[...] = total


def flush_kernel(chunks, *refs):
    n = len(chunks)
    sources, targets, bounces = refs[:n], refs[n : 2 * n], refs[2 * n : 3 * n]
    in_sem, out_sem = refs[3 * n :]
    steps = []
    for i in range(n):
        size = sources[i].shape[0] // chunks[i]
        for t in range(chunks[i]):
            at = pl.ds(t * size, size)
            k = len(steps)
            steps.append(
                (
                    pltpu.make_async_copy(sources[i].at[at], bounces[i].at[at], in_sem.at[k]),
                    pltpu.make_async_copy(bounces[i].at[at], targets[i].at[at], out_sem.at[k]),
                )
            )
    for load, _ in steps:
        load.start()
    for load, store in steps:
        load.wait()
        store.start()
    for _, store in steps:
        store.wait()


def flush(chunks, *arrays):
    where = pl.BlockSpec(memory_space=pl.ANY)
    return pl.pallas_call(
        functools.partial(flush_kernel, chunks),
        out_shape=tuple(jax.ShapeDtypeStruct(a.shape, a.dtype) for a in arrays),
        in_specs=[where] * len(arrays),
        out_specs=(where,) * len(arrays),
        scratch_shapes=[pltpu.VMEM(a.shape, a.dtype) for a in arrays]
        + [pltpu.SemaphoreType.DMA((sum(chunks),))] * 2,
        compiler_params=pltpu.CompilerParams(vmem_limit_bytes=60 << 20),
        name="flush",
    )(*arrays)


def body(
    queries, cotangent, cond, nbr_owner, nbr_block, database, lengths, gain, w_down, w_up, w_kv
):
    pools = lax.axis_size("pool")
    columns = lax.axis_size("dp")
    tokens, hq = queries.shape[2:]
    spans, width = cond.shape[2:]
    nbr = nbr_owner.shape[3]
    blocks, slot_len = database.shape[2:4]
    rank = w_down.shape[1]
    per = spans * nbr
    quarter = slot_len // pools
    live = (pools - 1) * per
    piece = width // (pools * columns)
    dma = pltpu.SemaphoreType.DMA
    vmem = pl.BlockSpec(memory_space=pltpu.VMEM)
    smem = pl.BlockSpec(memory_space=pltpu.SMEM)
    where = pl.BlockSpec(memory_space=pl.ANY)
    attn_out, q_grad, cond_grad, adapter_grad = pl.pallas_call(
        functools.partial(whole_kernel, pools, columns),
        out_shape=(
            jax.ShapeDtypeStruct((tokens, hq), BF16),
            jax.ShapeDtypeStruct((tokens, hq), BF16),
            jax.ShapeDtypeStruct((spans, width), F32),
            jax.ShapeDtypeStruct((piece, 2 * rank), F32),
        ),
        in_specs=[smem, smem, smem, where, where, where, vmem, vmem, where, where, where],
        out_specs=(where, where, vmem, vmem),
        scratch_shapes=[
            pltpu.VMEM((tokens, hq), BF16),
            pltpu.VMEM((tokens, hq), BF16),
            pltpu.VMEM((1, 128), jnp.int32),
            pltpu.VMEM((columns, pools, 1, 128), jnp.int32),
            pltpu.SMEM((columns, pools, 1, 128), jnp.int32),
            pltpu.VMEM((columns, 128), jnp.int32),
            pltpu.SMEM((columns, 128), jnp.int32),
            pltpu.SMEM((live,), jnp.int32),
            pltpu.SMEM((per,), jnp.int32),
            pltpu.VMEM((blocks, quarter, width), BF16),
            pltpu.VMEM((columns, 2, quarter, width), BF16),
            pltpu.VMEM((2 * columns, quarter, width), BF16),
            pltpu.VMEM((live, quarter, width), BF16),
            pltpu.VMEM((pools, per, quarter, width), BF16),
            pltpu.VMEM((tokens, hq), BF16),
            pltpu.VMEM((tokens, hq), BF16),
            pltpu.VMEM((width, rank), BF16),
            pltpu.VMEM((rank, width), BF16),
            pltpu.VMEM((width, 2 * hq), BF16),
            pltpu.VMEM((nbr * slot_len, 2 * hq), BF16),
            pltpu.VMEM((nbr * slot_len, 2 * hq), BF16),
            pltpu.VMEM((width, 2 * rank), F32),
            pltpu.VMEM((columns, pools, piece, 2 * rank), BF16),
            pltpu.VMEM((columns, pools, piece, 2 * rank), BF16),
            pltpu.VMEM((pools, piece, 2 * rank), F32),
            pltpu.VMEM((pools, piece, 2 * rank), F32),
            dma((5,)),
            dma((spans, 2)),
            dma((3,)),
            dma((2, pools)),
            dma((2,)),
            dma((pools,)),
            dma((pools,)),
            dma((columns,)),
            dma((columns,)),
            dma((columns,)),
            dma((columns,)),
            dma((spans, pools)),
            dma((spans, pools)),
            dma((columns,)),
            dma((columns,)),
            dma((pools,)),
            dma((pools,)),
        ],
        compiler_params=pltpu.CompilerParams(
            collective_id=0, has_side_effects=True, vmem_limit_bytes=60 << 20
        ),
        name="whole",
    )(
        nbr_owner.reshape(spans, nbr).T,
        nbr_block.reshape(spans, nbr).T,
        lengths.reshape(1, blocks),
        database.reshape(blocks, slot_len, width),
        queries.reshape(tokens, hq),
        cotangent.reshape(tokens, hq),
        cond.reshape(spans, width),
        gain.reshape(1, width),
        w_down,
        w_up,
        w_kv,
    )
    attn_out, q_grad, cond_grad, adapter_grad = flush(
        (4, 4, 1, 1), attn_out, q_grad, cond_grad, adapter_grad
    )
    return (
        attn_out.reshape(1, 1, tokens, hq),
        q_grad.reshape(1, 1, tokens, hq),
        cond_grad.reshape(1, 1, spans, width),
        adapter_grad,
    )


def solution(mesh):
    return jax.shard_map(
        body,
        mesh=mesh,
        in_specs=(
            P("pool", "dp", None, None),
            P("pool", "dp", None, None),
            P("pool", "dp", None, None),
            P("pool", "dp", None, None),
            P("pool", "dp", None, None),
            P("pool", "dp", None, None, None),
            P("pool", "dp", None),
            P(),
            P(),
            P(),
            P(),
        ),
        out_specs=(
            P("pool", "dp", None, None),
            P("pool", "dp", None, None),
            P("pool", "dp", None, None),
            P(("pool", "dp"), None),
        ),
        check_vma=False,
    )
```

```python
import functools

import jax
import jax.numpy as jnp
from jax import lax
from jax.experimental import pallas as pl
from jax.experimental.pallas import tpu as pltpu
from jax.sharding import PartitionSpec as P

HEAD = 128
SPAN = 64
EPSILON = 1e-06
FLOOR = -1e30
STAGE = 6
GRID = (4, 2, 4)
ORDER = ((3, 1, 1), (2, 0, 2), (1, 1, 0), (1, 0, 3), (3, 0, 3), (0, 0, 2), (0, 1, 2), (3, 1, 3), (1, 0, 0), (2, 0, 1), (1, 0, 2), (2, 1, 0), (3, 1, 2), (1, 1, 2), (2, 1, 2), (0, 0, 1), (2, 1, 1), (3, 0, 0), (0, 1, 3), (1, 1, 1), (2, 1, 3), (1, 1, 3), (2, 0, 0), (0, 1, 0), (1, 0, 1), (0, 0, 3), (3, 0, 1), (3, 0, 2), (3, 1, 0), (2, 0, 3), (0, 1, 1))
F32 = jnp.float32
BF16 = jnp.bfloat16
MESH = pl.DeviceIdType.MESH


def dot_nn(a, b):
    return lax.dot_general(a, b, (((1,), (0,)), ((), ())), preferred_element_type=F32)


def dot_nt(a, b):
    return lax.dot_general(a, b, (((1,), (1,)), ((), ())), preferred_element_type=F32)


def dot_tn(a, b):
    return lax.dot_general(a, b, (((0,), (0,)), ((), ())), preferred_element_type=F32)


def shifted(me, step):
    z, x, y = me // (GRID[1] * GRID[2]), lax.rem(me // GRID[2], GRID[1]), lax.rem(me, GRID[2])
    z, x, y = (lax.rem(c + d, n) for c, d, n in zip((z, x, y), step, GRID))
    return (z * GRID[1] + x) * GRID[2] + y


def greet(pools, columns):
    pool, me = lax.axis_index("pool"), lax.axis_index("dp")
    barrier = pltpu.get_barrier_semaphore()

    def hello(d, carry):
        pl.semaphore_signal(
            barrier, inc=1, device_id={"dp": lax.rem(me + d, columns)}, device_id_type=MESH
        )
        return carry

    lax.fori_loop(1, columns, hello, 0)
    for d in range(1, pools):
        pl.semaphore_signal(
            barrier, inc=1, device_id={"pool": lax.rem(pool + d, pools)}, device_id_type=MESH
        )
    pl.semaphore_wait(barrier, columns - 1 + pools - 1)


def whole_kernel(
    pools, columns,
    owner_ref, block_ref, len_ref, db_ref, q_hbm, do_hbm, cond_ref, gain_ref, wd_hbm, wu_hbm,
    wkv_hbm,
    out_hbm, dq_hbm, cg_ref, sum_ref,
    out_ref, dq_ref, row, metas, smeta, found, table, place, lens, share, send, got, pick, blk,
    q_ref, do_ref, wd_ref, wu_ref, wkv_ref, kv, kvg, ad_ref, part, lands, held, tops,
    load_sem, store_sem, local_sem, base_send, base_recv, row_send, row_recv, meta_send, meta_recv, hand_sem,
    slot_send, slot_recv, pick_send, pick_recv, a_send, a_recv, b_send, b_recv,
):
    pool, me = lax.axis_index("pool"), lax.axis_index("dp")
    top = pools - 1
    nbr, spans = owner_ref.shape
    per = spans * nbr
    blocks, quarter, width = share.shape
    hq = q_ref.shape[1]
    rank = wd_ref.shape[1]
    slot_len = pools * quarter
    is_enc = pool == top
    is_dec = jnp.logical_not(is_enc)

    loads = [
        pltpu.make_async_copy(a, b, load_sem.at[i])
        for i, (a, b) in enumerate(
            ((wd_hbm, wd_ref), (wu_hbm, wu_ref), (wkv_hbm, wkv_ref), (q_hbm, q_ref), (do_hbm, do_ref))
        )
    ]

    @pl.when(is_dec)
    def _():
        for load in loads:
            load.start()

    def each(action):
        def step(d, carry):
            action(d)
            return carry

        lax.fori_loop(1, columns, step, 0)

    lane = lax.broadcasted_iota(jnp.int32, (1, 128), 1)
    line = jnp.zeros((1, 128), jnp.int32)
    for k in range(per):
        line = jnp.where(lane == k, owner_ref[k % nbr, k // nbr], line)
        line = jnp.where(lane == per + k, block_ref[k % nbr, k // nbr], line)
    for k in range(blocks):
        line = jnp.where(lane == 2 * per + k, len_ref[0, k], line)
    row[...] = line

    @pl.when(is_dec)
    def _():
        metas[me, pool] = line

    greet(pools, columns)

    def row_copy(d):
        return pltpu.make_async_remote_copy(
            src_ref=row,
            dst_ref=metas.at[me, pool],
            send_sem=row_send.at[d],
            recv_sem=row_recv.at[pools - d],
            device_id={"pool": lax.rem(pool + d, pools)},
            device_id_type=MESH,
        )

    for d in range(1, pools):

        @pl.when(lax.rem(pool + d, pools) != top)
        def _():
            row_copy(d).start()

    early = blocks // 4
    halves = (pl.ds(0, early), pl.ds(early, blocks - early))

    def base_copy(p, half):
        return pltpu.make_async_remote_copy(
            src_ref=db_ref.at[halves[half], pl.ds(p * quarter, quarter), :],
            dst_ref=share.at[halves[half]],
            send_sem=base_send.at[half, p],
            recv_sem=base_recv.at[half],
            device_id={"pool": p},
            device_id_type=MESH,
        )

    base_own = pltpu.make_async_copy(
        db_ref.at[:, pl.ds(top * quarter, quarter), :], share, local_sem.at[0]
    )

    @pl.when(is_enc)
    def _():
        base_own.start()
        for p in (top - 1,) + tuple(range(top - 1)):
            for half in range(2):
                base_copy(p, half).start()

    for d in range(1, pools):

        @pl.when(lax.rem(pool + d, pools) != top)
        def _():
            row_copy(d).wait_send()

        @pl.when(is_dec)
        def _():
            row_copy(d).wait_recv()

    def meta_copy(d):
        return pltpu.make_async_remote_copy(
            src_ref=metas.at[me],
            dst_ref=metas.at[me],
            send_sem=meta_send.at[d],
            recv_sem=meta_recv.at[columns - d],
            device_id={"dp": lax.rem(me + d, columns)},
            device_id_type=MESH,
        )

    hand = pltpu.make_async_remote_copy(
        src_ref=metas,
        dst_ref=metas,
        send_sem=hand_sem.at[0],
        recv_sem=hand_sem.at[1],
        device_id={"pool": top},
        device_id_type=MESH,
    )

    @pl.when(is_dec)
    def _():
        each(lambda d: meta_copy(d).start())
        each(lambda d: meta_copy(d).wait())

    @pl.when(pool == top - 1)
    def _():
        hand.start()

    @pl.when(is_enc)
    def _():
        hand.wait_recv()

    to_scalar = pltpu.make_async_copy(metas, smeta, local_sem.at[1])

    lanes = lax.broadcasted_iota(jnp.int32, (columns, 128), 1)
    least = jnp.full((columns, 128), blocks << 16, jnp.int32)
    most = jnp.zeros((columns, 128), jnp.int32)
    for p in range(top):
        lists = metas[:, p, 0, :]
        key = (lanes + (p * per + 1)) * blocks + pltpu.roll(lists, 128 - per, 1)
        named = jnp.logical_and(lists == me, lanes < per)
        least = jnp.minimum(least, jnp.where(named, key, blocks << 16))
        most = jnp.maximum(most, jnp.where(named, key, 0))
    least = jnp.bitwise_and(jnp.min(least, axis=1, keepdims=True), blocks - 1)
    most = jnp.bitwise_and(jnp.max(most, axis=1, keepdims=True), blocks - 1)
    found[...] = jnp.where(lanes == 0, least, most)
    to_table = pltpu.make_async_copy(found, table, local_sem.at[2])
    to_table.start()
    to_table.wait()
    to_scalar.start()

    @pl.when(is_enc)
    def _():
        base_own.wait()

    @pl.when(is_dec)
    def _():
        base_copy(0, 0).wait_recv()
        base_copy(0, 1).wait_recv()

    def slot_copy(d):
        to = shifted(me, ORDER[d])
        return pltpu.make_async_remote_copy(
            src_ref=send.at[to],
            dst_ref=got.at[pl.ds(2 * me, 2)],
            send_sem=slot_send.at[d],
            recv_sem=slot_recv.at[d],
            device_id={"dp": to},
            device_id_type=MESH,
        )

    def fill(d):
        to = shifted(me, ORDER[d])
        for r in range(2):
            send[to, r] = share[table[to, r]]

    for d in range(columns - 1):
        fill(d)
        if d >= 2:
            slot_copy(d - 2).start()
    for r in range(2):
        got[2 * me + r] = share[table[me, r]]
    for d in range(columns - 3, columns - 1):
        slot_copy(d).start()

    @pl.when(pool == top - 1)
    def _():
        hand.wait_send()

    to_scalar.wait()
    names = [smeta[me, q // per, 0, q % per] for q in range(top * per)]
    for q in range(top * per):
        again = jnp.int32(0)
        for e in range(q):
            again = jnp.where(names[e] == names[q], 1, again)
        place[q] = 2 * names[q] + again
    mine = jnp.minimum(pool, top - 1)
    for k in range(per):
        lens[k] = smeta[smeta[me, mine, 0, k], top, 0, 2 * per + smeta[me, mine, 0, per + k]]

    ad_ref[...] = jnp.zeros_like(ad_ref)
    cg_ref[...] = jnp.zeros_like(cg_ref)

    def stores(c):
        at = pl.ds(pl.multiple_of(c * SPAN, SPAN), SPAN)
        return (
            pltpu.make_async_copy(out_ref.at[at], out_hbm.at[at], store_sem.at[c, 0]),
            pltpu.make_async_copy(dq_ref.at[at], dq_hbm.at[at], store_sem.at[c, 1]),
        )

    @pl.when(is_enc)
    def _():
        out_ref[...] = jnp.zeros_like(out_ref)
        dq_ref[...] = jnp.zeros_like(dq_ref)
        for p in range(top):
            for part_of in range(2):
                base_copy(p, part_of).wait_send()
        for c in range(spans):
            for store in stores(c):
                store.start()

    for d in range(columns - 1):
        slot_copy(d).wait_recv()

    def pick_copy(p, c):
        return pltpu.make_async_remote_copy(
            src_ref=pick.at[pl.ds(p * per + c * nbr, nbr)],
            dst_ref=blk.at[pool, pl.ds(c * nbr, nbr)],
            send_sem=pick_send.at[c, p],
            recv_sem=pick_recv.at[c, pool],
            device_id={"pool": p},
            device_id_type=MESH,
        )

    def pick_from(p, c):
        return pltpu.make_async_remote_copy(
            src_ref=pick.at[pl.ds(0, nbr)],
            dst_ref=blk.at[p, pl.ds(c * nbr, nbr)],
            send_sem=pick_send.at[c, p],
            recv_sem=pick_recv.at[c, p],
            device_id={"pool": p},
            device_id_type=MESH,
        )

    def choose(c):
        for n in range(nbr):
            k = c * nbr + n
            for p in range(top):
                pick[p * per + k] = got[place[p * per + k]]
            blk[pool, k] = got[place[mine * per + k]]

    def deliver(c):
        for p in range(top):

            @pl.when(pool != p)
            def _():
                pick_copy(p, c).start()

    choose(0)
    for c in range(1, spans):
        choose(c)
        deliver(c - 1)
    deliver(spans - 1)

    def span(c, carry):
        for p in range(pools):

            @pl.when(pool != p)
            def _():
                pick_from(p, c).wait_recv()

        @pl.when(c > 0)
        def _():
            for store in stores(c - 1):
                store.start()

        keys = nbr * slot_len
        scaling = HEAD ** (-0.5)
        at = pl.ds(pl.multiple_of(c * SPAN, SPAN), SPAN)
        rows = jnp.concatenate(
            [blk[p, c * nbr + n] for n in range(nbr) for p in range(pools)], axis=0
        ).astype(F32)
        cond = cond_ref[...].astype(F32)
        here = lax.broadcasted_iota(jnp.int32, cond.shape, 0) == c
        cond_row = jnp.sum(jnp.where(here, cond, 0.0), axis=0, keepdims=True)
        gain = gain_ref[...]
        x_full = rows + cond_row
        inv_rms = lax.rsqrt(jnp.mean(x_full * x_full, axis=-1, keepdims=True) + EPSILON)
        normed = x_full * inv_rms
        hidden = (normed * gain).astype(BF16)
        latent = dot_nn(hidden, wd_ref[...]).astype(BF16)
        encoded = (x_full + dot_nn(latent, wu_ref[...])).astype(BF16)
        for t in range(2 * hq // 512):
            cols = pl.ds(t * 512, 512)
            kv[:, cols] = dot_nn(encoded, wkv_ref[:, cols]).astype(BF16)

        slot = lax.broadcasted_iota(jnp.int32, (SPAN, keys), 1)
        bound = jnp.where(slot < slot_len, lens[c * nbr], lens[c * nbr + 1] + slot_len)
        usable = slot < bound

        def score(h):
            qs = pl.ds(h * HEAD, HEAD)
            vs = pl.ds(hq + h * HEAD, HEAD)
            s = dot_nt(q_ref[at, qs], kv[:, qs])
            dp = dot_nt(do_ref[at, qs], kv[:, vs])
            return s, dp

        def weigh(s, dp):
            s = jnp.where(usable, s * scaling, FLOOR)
            e = jnp.exp(s - jnp.max(s, axis=-1, keepdims=True))
            p = e * (1.0 / jnp.sum(e, axis=-1, keepdims=True))
            pdp = p * dp
            delta = jnp.sum(pdp, axis=-1, keepdims=True)
            return p.astype(BF16), (pdp - p * delta).astype(BF16)

        def finish(h, pb, ds):
            qs = pl.ds(h * HEAD, HEAD)
            vs = pl.ds(hq + h * HEAD, HEAD)
            out_ref[at, qs] = dot_nn(pb, kv[:, vs]).astype(BF16)
            dq_ref[at, qs] = (dot_nn(ds, kv[:, qs]) * scaling).astype(BF16)
            kvg[:, qs] = (dot_tn(ds, q_ref[at, qs]) * scaling).astype(BF16)
            kvg[:, vs] = dot_tn(pb, do_ref[at, qs]).astype(BF16)

        heads = hq // HEAD
        first, second = {}, {}
        for i in range(heads + 2 * STAGE):
            if i < heads:
                first[i] = score(i)
            if 0 <= i - STAGE < heads:
                second[i - STAGE] = weigh(*first.pop(i - STAGE))
            if 0 <= i - 2 * STAGE < heads:
                finish(i - 2 * STAGE, *second.pop(i - 2 * STAGE))

        enc_grad = dot_nt(kvg[...], wkv_ref[...]).astype(BF16)
        lat_grad = dot_nt(enc_grad, wu_ref[...]).astype(BF16)
        scaled = dot_nt(lat_grad, wd_ref[...]) * gain
        mean = jnp.mean(scaled * normed, axis=-1, keepdims=True)
        x_grad = enc_grad.astype(F32) + inv_rms * (scaled - normed * mean)
        cg_ref[pl.ds(c, 1), :] = jnp.sum(x_grad, axis=0, keepdims=True)
        ad_ref[:, :rank] += dot_tn(hidden, lat_grad)
        ad_ref[:, rank:] += dot_tn(enc_grad, latent)
        return carry

    def a_copy(d):
        to = shifted(me, ORDER[d])
        return pltpu.make_async_remote_copy(
            src_ref=part.at[to],
            dst_ref=lands.at[me],
            send_sem=a_send.at[d],
            recv_sem=a_recv.at[d],
            device_id={"dp": to},
            device_id_type=MESH,
        )

    def b_copy(p):
        return pltpu.make_async_remote_copy(
            src_ref=held.at[p],
            dst_ref=tops.at[pool],
            send_sem=b_send.at[p],
            recv_sem=b_recv.at[pool],
            device_id={"pool": p},
            device_id_type=MESH,
        )

    def b_from(p):
        return pltpu.make_async_remote_copy(
            src_ref=held.at[p],
            dst_ref=tops.at[p],
            send_sem=b_send.at[p],
            recv_sem=b_recv.at[p],
            device_id={"pool": p},
            device_id_type=MESH,
        )

    @pl.when(is_dec)
    def _():
        for load in loads:
            load.wait()
        lax.fori_loop(0, spans, span, 0)
        for store in stores(spans - 1):
            store.start()
        piece = part.shape[2]
        for j in range(columns):
            for p in range(pools):
                part[j, p] = ad_ref[pl.ds((p * columns + j) * piece, piece), :].astype(BF16)
        for d in range(columns - 1):
            a_copy(d).start()
        lands[me] = part[me]

    for c in range(spans):
        for store in stores(c):
            store.wait()

    for d in range(columns - 1):
        slot_copy(d).wait_send()
    for c in range(spans):
        for p in range(top):

            @pl.when(pool != p)
            def _():
                pick_copy(p, c).wait_send()

    @pl.when(is_dec)
    def _():
        for d in range(columns - 1):
            a_copy(d).wait()

        def add(j, total):
            return total + lands[j].astype(F32)

        held[...] = lax.fori_loop(1, columns, add, lands[0].astype(F32))
        for p in range(pools):

            @pl.when(pool != p)
            def _():
                b_copy(p).start()

            @pl.when(pool == p)
            def _():
                tops[p] = held[p]

        for p in range(pools):

            @pl.when(pool != p)
            def _():
                b_copy(p).wait_send()

    for p in range(top):

        @pl.when(pool != p)
        def _():
            b_from(p).wait_recv()

    total = tops[0]
    for p in range(1, top):
        total = total + tops[p]
    sum_ref[...] = total


def flush_kernel(chunks, *refs):
    n = len(chunks)
    sources, targets, bounces = refs[:n], refs[n : 2 * n], refs[2 * n : 3 * n]
    in_sem, out_sem = refs[3 * n :]
    steps = []
    for i in range(n):
        size = sources[i].shape[0] // chunks[i]
        for t in range(chunks[i]):
            at = pl.ds(t * size, size)
            k = len(steps)
            steps.append(
                (
                    pltpu.make_async_copy(sources[i].at[at], bounces[i].at[at], in_sem.at[k]),
                    pltpu.make_async_copy(bounces[i].at[at], targets[i].at[at], out_sem.at[k]),
                )
            )
    for load, _ in steps:
        load.start()
    for load, store in steps:
        load.wait()
        store.start()
    for _, store in steps:
        store.wait()


def flush(chunks, *arrays):
    where = pl.BlockSpec(memory_space=pl.ANY)
    return pl.pallas_call(
        functools.partial(flush_kernel, chunks),
        out_shape=tuple(jax.ShapeDtypeStruct(a.shape, a.dtype) for a in arrays),
        in_specs=[where] * len(arrays),
        out_specs=(where,) * len(arrays),
        scratch_shapes=[pltpu.VMEM(a.shape, a.dtype) for a in arrays]
        + [pltpu.SemaphoreType.DMA((sum(chunks),))] * 2,
        compiler_params=pltpu.CompilerParams(vmem_limit_bytes=60 << 20),
        name="flush",
    )(*arrays)


def body(
    queries, cotangent, cond, nbr_owner, nbr_block, database, lengths, gain, w_down, w_up, w_kv
):
    pools = lax.axis_size("pool")
    columns = lax.axis_size("dp")
    tokens, hq = queries.shape[2:]
    spans, width = cond.shape[2:]
    nbr = nbr_owner.shape[3]
    blocks, slot_len = database.shape[2:4]
    rank = w_down.shape[1]
    per = spans * nbr
    quarter = slot_len // pools
    live = (pools - 1) * per
    piece = width // (pools * columns)
    dma = pltpu.SemaphoreType.DMA
    vmem = pl.BlockSpec(memory_space=pltpu.VMEM)
    smem = pl.BlockSpec(memory_space=pltpu.SMEM)
    where = pl.BlockSpec(memory_space=pl.ANY)
    attn_out, q_grad, cond_grad, adapter_grad = pl.pallas_call(
        functools.partial(whole_kernel, pools, columns),
        out_shape=(
            jax.ShapeDtypeStruct((tokens, hq), BF16),
            jax.ShapeDtypeStruct((tokens, hq), BF16),
            jax.ShapeDtypeStruct((spans, width), F32),
            jax.ShapeDtypeStruct((piece, 2 * rank), F32),
        ),
        in_specs=[smem, smem, smem, where, where, where, vmem, vmem, where, where, where],
        out_specs=(where, where, vmem, vmem),
        scratch_shapes=[
            pltpu.VMEM((tokens, hq), BF16),
            pltpu.VMEM((tokens, hq), BF16),
            pltpu.VMEM((1, 128), jnp.int32),
            pltpu.VMEM((columns, pools, 1, 128), jnp.int32),
            pltpu.SMEM((columns, pools, 1, 128), jnp.int32),
            pltpu.VMEM((columns, 128), jnp.int32),
            pltpu.SMEM((columns, 128), jnp.int32),
            pltpu.SMEM((live,), jnp.int32),
            pltpu.SMEM((per,), jnp.int32),
            pltpu.VMEM((blocks, quarter, width), BF16),
            pltpu.VMEM((columns, 2, quarter, width), BF16),
            pltpu.VMEM((2 * columns, quarter, width), BF16),
            pltpu.VMEM((live, quarter, width), BF16),
            pltpu.VMEM((pools, per, quarter, width), BF16),
            pltpu.VMEM((tokens, hq), BF16),
            pltpu.VMEM((tokens, hq), BF16),
            pltpu.VMEM((width, rank), BF16),
            pltpu.VMEM((rank, width), BF16),
            pltpu.VMEM((width, 2 * hq), BF16),
            pltpu.VMEM((nbr * slot_len, 2 * hq), BF16),
            pltpu.VMEM((nbr * slot_len, 2 * hq), BF16),
            pltpu.VMEM((width, 2 * rank), F32),
            pltpu.VMEM((columns, pools, piece, 2 * rank), BF16),
            pltpu.VMEM((columns, pools, piece, 2 * rank), BF16),
            pltpu.VMEM((pools, piece, 2 * rank), F32),
            pltpu.VMEM((pools, piece, 2 * rank), F32),
            dma((5,)),
            dma((spans, 2)),
            dma((3,)),
            dma((2, pools)),
            dma((2,)),
            dma((pools,)),
            dma((pools,)),
            dma((columns,)),
            dma((columns,)),
            dma((2,)),
            dma((columns,)),
            dma((columns,)),
            dma((spans, pools)),
            dma((spans, pools)),
            dma((columns,)),
            dma((columns,)),
            dma((pools,)),
            dma((pools,)),
        ],
        compiler_params=pltpu.CompilerParams(
            collective_id=0, has_side_effects=True, vmem_limit_bytes=60 << 20
        ),
        name="whole",
    )(
        nbr_owner.reshape(spans, nbr).T,
        nbr_block.reshape(spans, nbr).T,
        lengths.reshape(1, blocks),
        database.reshape(blocks, slot_len, width),
        queries.reshape(tokens, hq),
        cotangent.reshape(tokens, hq),
        cond.reshape(spans, width),
        gain.reshape(1, width),
        w_down,
        w_up,
        w_kv,
    )
    attn_out, q_grad, cond_grad, adapter_grad = flush(
        (4, 4, 1, 1), attn_out, q_grad, cond_grad, adapter_grad
    )
    return (
        attn_out.reshape(1, 1, tokens, hq),
        q_grad.reshape(1, 1, tokens, hq),
        cond_grad.reshape(1, 1, spans, width),
        adapter_grad,
    )


def solution(mesh):
    return jax.shard_map(
        body,
        mesh=mesh,
        in_specs=(
            P("pool", "dp", None, None),
            P("pool", "dp", None, None),
            P("pool", "dp", None, None),
            P("pool", "dp", None, None),
            P("pool", "dp", None, None),
            P("pool", "dp", None, None, None),
            P("pool", "dp", None),
            P(),
            P(),
            P(),
            P(),
        ),
        out_specs=(
            P("pool", "dp", None, None),
            P("pool", "dp", None, None),
            P("pool", "dp", None, None),
            P(("pool", "dp"), None),
        ),
        check_vma=False,
    )
```

```python
import functools

import jax
import jax.numpy as jnp
from jax import lax
from jax.experimental import pallas as pl
from jax.experimental.pallas import tpu as pltpu
from jax.sharding import PartitionSpec as P

HEAD = 128
SPAN = 64
EPSILON = 1e-06
FLOOR = -1e30
STAGE = 6
GRID = (4, 2, 4)
ORDER = ((3, 1, 1), (2, 0, 2), (1, 1, 0), (1, 0, 3), (3, 0, 3), (0, 0, 2), (0, 1, 2), (3, 1, 3), (1, 0, 0), (2, 0, 1), (1, 0, 2), (2, 1, 0), (3, 1, 2), (1, 1, 2), (2, 1, 2), (0, 0, 1), (2, 1, 1), (3, 0, 0), (0, 1, 3), (1, 1, 1), (2, 1, 3), (1, 1, 3), (2, 0, 0), (0, 1, 0), (1, 0, 1), (0, 0, 3), (3, 0, 1), (3, 0, 2), (3, 1, 0), (2, 0, 3), (0, 1, 1))
F32 = jnp.float32
BF16 = jnp.bfloat16
MESH = pl.DeviceIdType.MESH


def dot_nn(a, b):
    return lax.dot_general(a, b, (((1,), (0,)), ((), ())), preferred_element_type=F32)


def dot_nt(a, b):
    return lax.dot_general(a, b, (((1,), (1,)), ((), ())), preferred_element_type=F32)


def dot_tn(a, b):
    return lax.dot_general(a, b, (((0,), (0,)), ((), ())), preferred_element_type=F32)


def shifted(me, step):
    z, x, y = me // (GRID[1] * GRID[2]), lax.rem(me // GRID[2], GRID[1]), lax.rem(me, GRID[2])
    z, x, y = (lax.rem(c + d, n) for c, d, n in zip((z, x, y), step, GRID))
    return (z * GRID[1] + x) * GRID[2] + y


def greet(pools, columns):
    pool, me = lax.axis_index("pool"), lax.axis_index("dp")
    barrier = pltpu.get_barrier_semaphore()

    def hello(d, carry):
        pl.semaphore_signal(
            barrier, inc=1, device_id={"dp": lax.rem(me + d, columns)}, device_id_type=MESH
        )
        return carry

    lax.fori_loop(1, columns, hello, 0)
    for d in range(1, pools):
        pl.semaphore_signal(
            barrier, inc=1, device_id={"pool": lax.rem(pool + d, pools)}, device_id_type=MESH
        )
    pl.semaphore_wait(barrier, columns - 1 + pools - 1)


def whole_kernel(
    pools, columns,
    owner_ref, block_ref, len_ref, db_ref, q_hbm, do_hbm, cond_ref, gain_ref, wd_hbm, wu_hbm,
    wkv_hbm,
    out_hbm, dq_hbm, cg_ref, sum_ref,
    out_ref, dq_ref, row, metas, smeta, found, table, place, lens, share, send, got, pick, blk,
    q_ref, do_ref, wd_ref, wu_ref, wkv_ref, kv, kvg, ad_ref, part, lands, held, tops,
    load_sem, store_sem, local_sem, base_send, base_recv, row_send, row_recv, meta_send, meta_recv, hand_sem,
    slot_send, slot_recv, pick_send, pick_recv, a_send, a_recv, b_send, b_recv,
):
    pool, me = lax.axis_index("pool"), lax.axis_index("dp")
    top = pools - 1
    nbr, spans = owner_ref.shape
    per = spans * nbr
    blocks, quarter, width = share.shape
    hq = q_ref.shape[1]
    rank = wd_ref.shape[1]
    slot_len = pools * quarter
    is_enc = pool == top
    is_dec = jnp.logical_not(is_enc)

    loads = [
        pltpu.make_async_copy(a, b, load_sem.at[i])
        for i, (a, b) in enumerate(
            ((wd_hbm, wd_ref), (wu_hbm, wu_ref), (wkv_hbm, wkv_ref), (q_hbm, q_ref), (do_hbm, do_ref))
        )
    ]

    @pl.when(is_dec)
    def _():
        for load in loads:
            load.start()

    def each(action):
        def step(d, carry):
            action(d)
            return carry

        lax.fori_loop(1, columns, step, 0)

    lane = lax.broadcasted_iota(jnp.int32, (1, 128), 1)
    line = jnp.zeros((1, 128), jnp.int32)
    for k in range(per):
        line = jnp.where(lane == k, owner_ref[k % nbr, k // nbr], line)
        line = jnp.where(lane == per + k, block_ref[k % nbr, k // nbr], line)
    for k in range(blocks):
        line = jnp.where(lane == 2 * per + k, len_ref[0, k], line)
    row[...] = line

    @pl.when(is_dec)
    def _():
        metas[me, pool] = line

    greet(pools, columns)

    def row_copy(d):
        return pltpu.make_async_remote_copy(
            src_ref=row,
            dst_ref=metas.at[me, pool],
            send_sem=row_send.at[d],
            recv_sem=row_recv.at[pools - d],
            device_id={"pool": lax.rem(pool + d, pools)},
            device_id_type=MESH,
        )

    for d in range(1, pools):

        @pl.when(lax.rem(pool + d, pools) != top)
        def _():
            row_copy(d).start()

    early = blocks // 4
    halves = (pl.ds(0, early), pl.ds(early, blocks - early))

    def base_copy(p, half):
        return pltpu.make_async_remote_copy(
            src_ref=db_ref.at[halves[half], pl.ds(p * quarter, quarter), :],
            dst_ref=share.at[halves[half]],
            send_sem=base_send.at[half, p],
            recv_sem=base_recv.at[half],
            device_id={"pool": p},
            device_id_type=MESH,
        )

    base_own = pltpu.make_async_copy(
        db_ref.at[:, pl.ds(top * quarter, quarter), :], share, local_sem.at[0]
    )

    @pl.when(is_enc)
    def _():
        base_own.start()
        for p in (top - 1,) + tuple(range(top - 1)):
            for half in range(2):
                base_copy(p, half).start()

    for d in range(1, pools):

        @pl.when(lax.rem(pool + d, pools) != top)
        def _():
            row_copy(d).wait_send()

        @pl.when(is_dec)
        def _():
            row_copy(d).wait_recv()

    def meta_copy(d):
        return pltpu.make_async_remote_copy(
            src_ref=metas.at[me],
            dst_ref=metas.at[me],
            send_sem=meta_send.at[d],
            recv_sem=meta_recv.at[columns - d],
            device_id={"dp": lax.rem(me + d, columns)},
            device_id_type=MESH,
        )

    hand = pltpu.make_async_remote_copy(
        src_ref=metas,
        dst_ref=metas,
        send_sem=hand_sem.at[0],
        recv_sem=hand_sem.at[1],
        device_id={"pool": top},
        device_id_type=MESH,
    )

    @pl.when(is_dec)
    def _():
        each(lambda d: meta_copy(d).start())
        each(lambda d: meta_copy(d).wait())

    @pl.when(pool == top - 1)
    def _():
        hand.start()

    @pl.when(is_enc)
    def _():
        hand.wait_recv()

    to_scalar = pltpu.make_async_copy(metas, smeta, local_sem.at[1])

    lanes = lax.broadcasted_iota(jnp.int32, (columns, 128), 1)
    least = jnp.full((columns, 128), blocks << 16, jnp.int32)
    most = jnp.zeros((columns, 128), jnp.int32)
    for p in range(top):
        lists = metas[:, p, 0, :]
        key = (lanes + (p * per + 1)) * blocks + pltpu.roll(lists, 128 - per, 1)
        named = jnp.logical_and(lists == me, lanes < per)
        least = jnp.minimum(least, jnp.where(named, key, blocks << 16))
        most = jnp.maximum(most, jnp.where(named, key, 0))
    least = jnp.bitwise_and(jnp.min(least, axis=1, keepdims=True), blocks - 1)
    most = jnp.bitwise_and(jnp.max(most, axis=1, keepdims=True), blocks - 1)
    found[...] = jnp.where(lanes == 0, least, most)
    to_table = pltpu.make_async_copy(found, table, local_sem.at[2])
    to_table.start()
    to_table.wait()
    to_scalar.start()

    @pl.when(is_enc)
    def _():
        base_own.wait()

    @pl.when(is_dec)
    def _():
        base_copy(0, 0).wait_recv()
        base_copy(0, 1).wait_recv()

    def slot_copy(d):
        to = shifted(me, ORDER[d])
        return pltpu.make_async_remote_copy(
            src_ref=send.at[to],
            dst_ref=got.at[pl.ds(2 * me, 2)],
            send_sem=slot_send.at[d],
            recv_sem=slot_recv.at[d],
            device_id={"dp": to},
            device_id_type=MESH,
        )

    def fill(d):
        to = shifted(me, ORDER[d])
        for r in range(2):
            send[to, r] = share[table[to, r]]

    for d in range(columns - 1):
        fill(d)
        if d >= 2:
            slot_copy(d - 2).start()
    for r in range(2):
        got[2 * me + r] = share[table[me, r]]
    for d in range(columns - 3, columns - 1):
        slot_copy(d).start()

    @pl.when(pool == top - 1)
    def _():
        hand.wait_send()

    to_scalar.wait()
    names = [smeta[me, q // per, 0, q % per] for q in range(top * per)]
    for q in range(top * per):
        again = jnp.int32(0)
        for e in range(q):
            again = jnp.where(names[e] == names[q], 1, again)
        place[q] = 2 * names[q] + again
    mine = jnp.minimum(pool, top - 1)
    for k in range(per):
        lens[k] = smeta[smeta[me, mine, 0, k], top, 0, 2 * per + smeta[me, mine, 0, per + k]]

    ad_ref[...] = jnp.zeros_like(ad_ref)
    cg_ref[...] = jnp.zeros_like(cg_ref)

    def stores(c):
        at = pl.ds(pl.multiple_of(c * SPAN, SPAN), SPAN)
        return (
            pltpu.make_async_copy(out_ref.at[at], out_hbm.at[at], store_sem.at[c, 0]),
            pltpu.make_async_copy(dq_ref.at[at], dq_hbm.at[at], store_sem.at[c, 1]),
        )

    @pl.when(is_enc)
    def _():
        out_ref[...] = jnp.zeros_like(out_ref)
        dq_ref[...] = jnp.zeros_like(dq_ref)
        for p in range(top):
            for part_of in range(2):
                base_copy(p, part_of).wait_send()
        for c in range(spans):
            for store in stores(c):
                store.start()

    for d in range(columns - 1):
        slot_copy(d).wait_recv()

    def pick_copy(p, c):
        return pltpu.make_async_remote_copy(
            src_ref=pick.at[pl.ds(p * per + c * nbr, nbr)],
            dst_ref=blk.at[pool, pl.ds(c * nbr, nbr)],
            send_sem=pick_send.at[c, p],
            recv_sem=pick_recv.at[c, pool],
            device_id={"pool": p},
            device_id_type=MESH,
        )

    def pick_from(p, c):
        return pltpu.make_async_remote_copy(
            src_ref=pick.at[pl.ds(0, nbr)],
            dst_ref=blk.at[p, pl.ds(c * nbr, nbr)],
            send_sem=pick_send.at[c, p],
            recv_sem=pick_recv.at[c, p],
            device_id={"pool": p},
            device_id_type=MESH,
        )

    def choose(c):
        for n in range(nbr):
            k = c * nbr + n
            for p in range(top):
                pick[p * per + k] = got[place[p * per + k]]
            blk[pool, k] = got[place[mine * per + k]]

    def deliver(c):
        for p in range(top):

            @pl.when(pool != p)
            def _():
                pick_copy(p, c).start()

    choose(0)
    for c in range(1, spans):
        choose(c)
        deliver(c - 1)
    deliver(spans - 1)

    def span(c, carry):
        for p in range(pools):

            @pl.when(pool != p)
            def _():
                pick_from(p, c).wait_recv()

        @pl.when(c > 0)
        def _():
            for store in stores(c - 1):
                store.start()

        keys = nbr * slot_len
        scaling = HEAD ** (-0.5)
        at = pl.ds(pl.multiple_of(c * SPAN, SPAN), SPAN)
        rows = jnp.concatenate(
            [blk[p, c * nbr + n] for n in range(nbr) for p in range(pools)], axis=0
        ).astype(F32)
        cond = cond_ref[...].astype(F32)
        here = lax.broadcasted_iota(jnp.int32, cond.shape, 0) == c
        cond_row = jnp.sum(jnp.where(here, cond, 0.0), axis=0, keepdims=True)
        gain = gain_ref[...]
        x_full = rows + cond_row
        inv_rms = lax.rsqrt(jnp.mean(x_full * x_full, axis=-1, keepdims=True) + EPSILON)
        normed = x_full * inv_rms
        hidden = (normed * gain).astype(BF16)
        latent = dot_nn(hidden, wd_ref[...]).astype(BF16)
        encoded = (x_full + dot_nn(latent, wu_ref[...])).astype(BF16)
        for t in range(2 * hq // 512):
            cols = pl.ds(t * 512, 512)
            kv[:, cols] = dot_nn(encoded, wkv_ref[:, cols]).astype(BF16)

        slot = lax.broadcasted_iota(jnp.int32, (SPAN, keys), 1)
        bound = jnp.where(slot < slot_len, lens[c * nbr], lens[c * nbr + 1] + slot_len)
        usable = slot < bound

        def score(h):
            qs = pl.ds(h * HEAD, HEAD)
            vs = pl.ds(hq + h * HEAD, HEAD)
            s = dot_nt(q_ref[at, qs], kv[:, qs])
            dp = dot_nt(do_ref[at, qs], kv[:, vs])
            return s, dp

        def weigh(s, dp):
            s = jnp.where(usable, s * scaling, FLOOR)
            e = jnp.exp(s - jnp.max(s, axis=-1, keepdims=True))
            p = e * (1.0 / jnp.sum(e, axis=-1, keepdims=True))
            pdp = p * dp
            delta = jnp.sum(pdp, axis=-1, keepdims=True)
            return p.astype(BF16), (pdp - p * delta).astype(BF16)

        def finish(h, pb, ds):
            qs = pl.ds(h * HEAD, HEAD)
            vs = pl.ds(hq + h * HEAD, HEAD)
            out_ref[at, qs] = dot_nn(pb, kv[:, vs]).astype(BF16)
            dq_ref[at, qs] = (dot_nn(ds, kv[:, qs]) * scaling).astype(BF16)
            kvg[:, qs] = (dot_tn(ds, q_ref[at, qs]) * scaling).astype(BF16)
            kvg[:, vs] = dot_tn(pb, do_ref[at, qs]).astype(BF16)

        heads = hq // HEAD
        first, second = {}, {}
        for i in range(heads + 2 * STAGE):
            if i < heads:
                first[i] = score(i)
            if 0 <= i - STAGE < heads:
                second[i - STAGE] = weigh(*first.pop(i - STAGE))
            if 0 <= i - 2 * STAGE < heads:
                finish(i - 2 * STAGE, *second.pop(i - 2 * STAGE))

        enc_grad = dot_nt(kvg[...], wkv_ref[...]).astype(BF16)
        lat_grad = dot_nt(enc_grad, wu_ref[...]).astype(BF16)
        scaled = dot_nt(lat_grad, wd_ref[...]) * gain
        mean = jnp.mean(scaled * normed, axis=-1, keepdims=True)
        x_grad = enc_grad.astype(F32) + inv_rms * (scaled - normed * mean)
        cg_ref[pl.ds(c, 1), :] = jnp.sum(x_grad, axis=0, keepdims=True)
        ad_ref[:, :rank] += dot_tn(hidden, lat_grad)
        ad_ref[:, rank:] += dot_tn(enc_grad, latent)
        return carry

    def a_copy(d):
        to = shifted(me, ORDER[d])
        return pltpu.make_async_remote_copy(
            src_ref=part.at[to],
            dst_ref=lands.at[me],
            send_sem=a_send.at[d],
            recv_sem=a_recv.at[d],
            device_id={"dp": to},
            device_id_type=MESH,
        )

    def b_copy(p):
        return pltpu.make_async_remote_copy(
            src_ref=held.at[p],
            dst_ref=tops.at[pool],
            send_sem=b_send.at[p],
            recv_sem=b_recv.at[pool],
            device_id={"pool": p},
            device_id_type=MESH,
        )

    def b_from(p):
        return pltpu.make_async_remote_copy(
            src_ref=held.at[p],
            dst_ref=tops.at[p],
            send_sem=b_send.at[p],
            recv_sem=b_recv.at[p],
            device_id={"pool": p},
            device_id_type=MESH,
        )

    @pl.when(is_dec)
    def _():
        for load in loads:
            load.wait()
        lax.fori_loop(0, spans, span, 0)
        for store in stores(spans - 1):
            store.start()
        piece = part.shape[2]
        for j in range(columns):
            for p in range(pools):
                part[j, p] = ad_ref[pl.ds((p * columns + j) * piece, piece), :].astype(BF16)
        for d in range(columns - 1):
            a_copy(d).start()
        lands[me] = part[me]

    for c in range(spans):
        for store in stores(c):
            store.wait()

    for d in range(columns - 1):
        slot_copy(d).wait_send()
    for c in range(spans):
        for p in range(top):

            @pl.when(pool != p)
            def _():
                pick_copy(p, c).wait_send()

    @pl.when(is_dec)
    def _():
        for d in range(columns - 1):
            a_copy(d).wait()

        def add(j, total):
            return total + lands[j].astype(F32)

        held[...] = lax.fori_loop(1, columns, add, lands[0].astype(F32))
        for p in range(pools):

            @pl.when(pool != p)
            def _():
                b_copy(p).start()

            @pl.when(pool == p)
            def _():
                tops[p] = held[p]

        for p in range(pools):

            @pl.when(pool != p)
            def _():
                b_copy(p).wait_send()

    for p in range(top):

        @pl.when(pool != p)
        def _():
            b_from(p).wait_recv()

    total = tops[0]
    for p in range(1, top):
        total = total + tops[p]
    sum_ref[...] = total


def flush_kernel(chunks, *refs):
    n = len(chunks)
    sources, targets, bounces = refs[:n], refs[n : 2 * n], refs[2 * n : 3 * n]
    in_sem, out_sem = refs[3 * n :]
    steps = []
    for i in range(n):
        size = sources[i].shape[0] // chunks[i]
        for t in range(chunks[i]):
            at = pl.ds(t * size, size)
            k = len(steps)
            steps.append(
                (
                    pltpu.make_async_copy(sources[i].at[at], bounces[i].at[at], in_sem.at[k]),
                    pltpu.make_async_copy(bounces[i].at[at], targets[i].at[at], out_sem.at[k]),
                )
            )
    for load, _ in steps:
        load.start()
    for load, store in steps:
        load.wait()
        store.start()
    for _, store in steps:
        store.wait()


def flush(chunks, *arrays):
    where = pl.BlockSpec(memory_space=pl.ANY)
    return pl.pallas_call(
        functools.partial(flush_kernel, chunks),
        out_shape=tuple(jax.ShapeDtypeStruct(a.shape, a.dtype) for a in arrays),
        in_specs=[where] * len(arrays),
        out_specs=(where,) * len(arrays),
        scratch_shapes=[pltpu.VMEM(a.shape, a.dtype) for a in arrays]
        + [pltpu.SemaphoreType.DMA((sum(chunks),))] * 2,
        compiler_params=pltpu.CompilerParams(vmem_limit_bytes=60 << 20),
        name="flush",
    )(*arrays)


def body(
    queries, cotangent, cond, nbr_owner, nbr_block, database, lengths, gain, w_down, w_up, w_kv
):
    pools = lax.axis_size("pool")
    columns = lax.axis_size("dp")
    tokens, hq = queries.shape[2:]
    spans, width = cond.shape[2:]
    nbr = nbr_owner.shape[3]
    blocks, slot_len = database.shape[2:4]
    rank = w_down.shape[1]
    per = spans * nbr
    quarter = slot_len // pools
    live = (pools - 1) * per
    piece = width // (pools * columns)
    dma = pltpu.SemaphoreType.DMA
    vmem = pl.BlockSpec(memory_space=pltpu.VMEM)
    smem = pl.BlockSpec(memory_space=pltpu.SMEM)
    where = pl.BlockSpec(memory_space=pl.ANY)
    attn_out, q_grad, cond_grad, adapter_grad = pl.pallas_call(
        functools.partial(whole_kernel, pools, columns),
        out_shape=(
            jax.ShapeDtypeStruct((tokens, hq), BF16),
            jax.ShapeDtypeStruct((tokens, hq), BF16),
            jax.ShapeDtypeStruct((spans, width), F32),
            jax.ShapeDtypeStruct((piece, 2 * rank), F32),
        ),
        in_specs=[smem, smem, smem, where, where, where, vmem, vmem, where, where, where],
        out_specs=(where, where, vmem, vmem),
        scratch_shapes=[
            pltpu.VMEM((tokens, hq), BF16),
            pltpu.VMEM((tokens, hq), BF16),
            pltpu.VMEM((1, 128), jnp.int32),
            pltpu.VMEM((columns, pools, 1, 128), jnp.int32),
            pltpu.SMEM((columns, pools, 1, 128), jnp.int32),
            pltpu.VMEM((columns, 128), jnp.int32),
            pltpu.SMEM((columns, 128), jnp.int32),
            pltpu.SMEM((live,), jnp.int32),
            pltpu.SMEM((per,), jnp.int32),
            pltpu.VMEM((blocks, quarter, width), BF16),
            pltpu.VMEM((columns, 2, quarter, width), BF16),
            pltpu.VMEM((2 * columns, quarter, width), BF16),
            pltpu.VMEM((live, quarter, width), BF16),
            pltpu.VMEM((pools, per, quarter, width), BF16),
            pltpu.VMEM((tokens, hq), BF16),
            pltpu.VMEM((tokens, hq), BF16),
            pltpu.VMEM((width, rank), BF16),
            pltpu.VMEM((rank, width), BF16),
            pltpu.VMEM((width, 2 * hq), BF16),
            pltpu.VMEM((nbr * slot_len, 2 * hq), BF16),
            pltpu.VMEM((nbr * slot_len, 2 * hq), BF16),
            pltpu.VMEM((width, 2 * rank), F32),
            pltpu.VMEM((columns, pools, piece, 2 * rank), BF16),
            pltpu.VMEM((columns, pools, piece, 2 * rank), BF16),
            pltpu.VMEM((pools, piece, 2 * rank), F32),
            pltpu.VMEM((pools, piece, 2 * rank), F32),
            dma((5,)),
            dma((spans, 2)),
            dma((3,)),
            dma((2, pools)),
            dma((2,)),
            dma((pools,)),
            dma((pools,)),
            dma((columns,)),
            dma((columns,)),
            dma((2,)),
            dma((columns,)),
            dma((columns,)),
            dma((spans, pools)),
            dma((spans, pools)),
            dma((columns,)),
            dma((columns,)),
            dma((pools,)),
            dma((pools,)),
        ],
        compiler_params=pltpu.CompilerParams(
            collective_id=0, has_side_effects=True, vmem_limit_bytes=60 << 20
        ),
        name="whole",
    )(
        nbr_owner.reshape(spans, nbr).T,
        nbr_block.reshape(spans, nbr).T,
        lengths.reshape(1, blocks),
        database.reshape(blocks, slot_len, width),
        queries.reshape(tokens, hq),
        cotangent.reshape(tokens, hq),
        cond.reshape(spans, width),
        gain.reshape(1, width),
        w_down,
        w_up,
        w_kv,
    )
    attn_out, q_grad, cond_grad, adapter_grad = flush(
        (8, 8, 1, 1), attn_out, q_grad, cond_grad, adapter_grad
    )
    return (
        attn_out.reshape(1, 1, tokens, hq),
        q_grad.reshape(1, 1, tokens, hq),
        cond_grad.reshape(1, 1, spans, width),
        adapter_grad,
    )


def solution(mesh):
    return jax.shard_map(
        body,
        mesh=mesh,
        in_specs=(
            P("pool", "dp", None, None),
            P("pool", "dp", None, None),
            P("pool", "dp", None, None),
            P("pool", "dp", None, None),
            P("pool", "dp", None, None),
            P("pool", "dp", None, None, None),
            P("pool", "dp", None),
            P(),
            P(),
            P(),
            P(),
        ),
        out_specs=(
            P("pool", "dp", None, None),
            P("pool", "dp", None, None),
            P("pool", "dp", None, None),
            P(("pool", "dp"), None),
        ),
        check_vma=False,
    )
```
